256 devices in a mesh: section: 8 (over z), expert: 32 (over y, x, core).
Axes of the slice: x: 4, y: 4, z: 8, core: 2. Of those that a mesh axis runs over, the one named last changes fastest.
Arguments:
- forward_in: bfloat16 [8, 512, 7168], P('section', 'expert'), may hold values from -6 to 6
- reverse_in: bfloat16 [8, 512, 7168], P('section', 'expert'), may hold values from -6 to 6
- norm_gain: bfloat16 [8, 7168], P('section'), may hold values from 0.099609375 to 1.8984375
- gate_up_weight: bfloat16 [8, 2, 7168, 8192], P('section', None, None, 'expert'), may hold values from -0.0625 to 0.0625
- down_weight: bfloat16 [8, 8192, 7168], P('section', 'expert'), may hold values from -0.125 to 0.125
- expert_ids: int32 [8, 2, 2, 512, 1], P('section', None, None, 'expert'), may hold values from 0 to 3; in each aligned block of 16 rows (0 to 15, 16 to 31, ..., all dimensions but the last counted through in order) at most 6 rows name the same one
- gate_weights: float32 [8, 2, 2, 512, 1], P('section', None, None, 'expert'), may hold values from 0.2 to 1
Outputs:
- forward_out: bfloat16 [8, 512, 7168], P('section', 'expert')
- reverse_out: bfloat16 [8, 512, 7168], P('section', 'expert')
The draws below stay inside these ranges and needn't reach their ends.
Inputs may be any that keep to these rules, and one draw needn't show every extreme that they name: `expert_ids`: in every layer, step and direction, the 16 tokens of one device name any one expert at most 6 times, and in some of these blocks one expert is named exactly 6 times. Each token names exactly one expert.
All inputs are finite; a program needn't handle non-finite values.
Results may differ from the reference program's by a relative error of at most 0.0075.
Values may be sent and summed in bfloat16 or wider, within the bound.
A program may use at most 128 MiB of HBM per device.

```python
import math
import jax
import jax.numpy as jnp
import numpy as np
from jax import lax

D = 7168
FF = 2048
EXPERTS = 4
TOP = 1
TICKS = 2
TOK_DEV = 16
SECTIONS = 8
TOKENS = 512
UNITS = 256
MOST = 6


def levels(stream_key, dims, split, least, largest):
    def one(position, blocks):
        heights = jax.random.uniform(jax.random.fold_in(jax.random.fold_in(stream_key, 6), position), (blocks,), jnp.float32, least / len(split), largest / len(split))
        return jnp.repeat(jnp.exp(heights), dims[position] // blocks).reshape((-1,) + (1,) * (len(dims) - position - 1))

    factor_of = one(*split[0])
    for cut in split[1:]:
        factor_of = factor_of * one(*cut)
    return factor_of


def assign_block(stream_key, own, number, rows, amount, top, reach, slope):
    ranking = jax.random.permutation(stream_key, amount)
    packed, ordinary = load_shares(amount, rows * top, reach, slope, True), load_shares(amount, rows * top, reach, slope, False)
    places = jnp.arange(amount)

    def named(sizes, rotation):
        used = int((sizes > 0).sum())
        fixed = max(1, used // 4)
        passed = fixed + (places - fixed + rotation * (used - fixed)) % max(1, amount - fixed)
        return jnp.zeros((amount,), jnp.int32).at[ranking[jnp.where(places < fixed, places, passed)]].set(jnp.asarray(sizes, jnp.int32))

    sizes = jnp.where(number % 4 == 0, named(packed, number // 4), named(ordinary, number - number // 4 - 1))
    mixed = jax.random.permutation(jax.random.fold_in(own, 3), amount)
    donor, taker = mixed[0:amount // 2 * 2:2], mixed[1:amount // 2 * 2:2]
    slack = jnp.minimum(sizes[donor] - 1, reach - sizes[taker]) // 2
    slack = jnp.where((donor == ranking[0]) | (taker == ranking[0]) | (sizes[taker] == 0), 0, jnp.maximum(slack, 0))
    passed = jax.random.randint(jax.random.fold_in(own, 4), (amount // 2,), 0, 1 << 20) % (slack + 1)
    sizes = sizes.at[donor].add(-passed).at[taker].add(passed)
    members = jnp.searchsorted(jnp.cumsum(sizes), jnp.arange(rows * top), side="right").astype(jnp.int32)
    listing = members.reshape(top, rows).T
    listing = listing[jax.random.permutation(jax.random.fold_in(own, 1), rows)]
    rotation = jax.random.randint(jax.random.fold_in(own, 2), (rows, 1), 0, top)
    return jnp.take_along_axis(listing, (jnp.arange(top)[None, :] + rotation) % top, axis=1)


def load_shares(number_of, total, reach, lean, full):
    portions = [(1 << 20) // math.isqrt(rank ** lean) + 1 for rank in range(1, number_of + 1)]
    largest = reach if full else min(reach, max(-(-total // number_of), total * portions[0] // sum(portions)))
    least = 1 if total - largest >= number_of - 1 else 0
    holding, spare = [largest] + [least] * (number_of - 1), total - largest - least * (number_of - 1)
    while spare > 0:
        free = [i for i in range(1, number_of) if holding[i] < largest] or [i for i in range(1, number_of) if holding[i] < reach]
        mass, left = sum([portions[i] for i in free]), spare
        for i in free:
            extra = min(reach - holding[i], max(1, left * portions[i] // mass), spare)
            holding[i] = holding[i] + extra
            spare = spare - extra
    return np.array(holding)


def bell_draw(rng, extent, deviation, most, shards=(), kind=jnp.bfloat16):
    entries = deviation * jax.random.normal(rng, extent, jnp.float32)
    if shards:
        entries = entries * levels(rng, extent, shards, -0.22, 0.18)
    return jnp.clip(entries, -most, most).astype(kind)


def setup_inputs(seed: int = 0) -> dict:
    keys = jax.random.split(jax.random.key(seed), 8)
    forward_in = bell_draw(keys[0], (SECTIONS, TOKENS, D), 1.0, 6.0, ((0, 8), (1, 32)))
    reverse_in = bell_draw(keys[1], (SECTIONS, TOKENS, D), 1.0, 6.0, ((0, 8), (1, 32)))
    norm_gain = jnp.clip(1.0 + 0.18 * jax.random.normal(keys[2], (SECTIONS, D), jnp.float32), 0.099609375, 1.8984375).astype(jnp.bfloat16)
    gate_up_weight = bell_draw(keys[3], (SECTIONS, 2, D, EXPERTS * FF), D ** -0.5, 0.0625, ((0, 8), (3, 32)))
    down_weight = bell_draw(keys[4], (SECTIONS, EXPERTS * FF, D), FF ** -0.5, 0.125, ((0, 8), (1, 32)))
    expert_ids_keys = jax.random.split(jax.random.fold_in(keys[5], 1), SECTIONS * TICKS * 2 * TOKENS // TOK_DEV)
    expert_ids_turns = jax.random.permutation(jax.random.fold_in(keys[5], 3), SECTIONS * TICKS * 2 * TOKENS // TOK_DEV)
    expert_ids = jax.vmap(lambda own, number: assign_block(jax.random.fold_in(keys[5], 2), own, number, TOK_DEV, EXPERTS, TOP, MOST, 2))(expert_ids_keys, expert_ids_turns).reshape((SECTIONS, TICKS, 2, TOKENS, TOP))
    gate_weights = jnp.clip(0.2 + 0.8 * jax.random.uniform(keys[6], (SECTIONS, TICKS, 2, TOKENS, TOP), jnp.float32) ** levels(keys[6], (SECTIONS, TICKS, 2, TOKENS, TOP), ((0, 8), (3, 32)), -0.2, 0.2), 0.2, 1.0)
    return dict(forward_in=forward_in, reverse_in=reverse_in, norm_gain=norm_gain, gate_up_weight=gate_up_weight, down_weight=down_weight, expert_ids=expert_ids, gate_weights=gate_weights)


def apply_layer(rows_in, gain, weight_in, weight_out, routes, shares):
    count = rows_in.shape[0]
    blocks = FF // UNITS
    rows_float = rows_in.astype(jnp.float32)
    scale = lax.rsqrt(lax.optimization_barrier(jnp.mean(rows_float * rows_float, axis=-1, keepdims=True)) + 1e-06)
    normed = (rows_float * scale * gain.astype(jnp.float32)).astype(jnp.bfloat16)
    total = rows_float
    for expert in range(EXPERTS):
        start = expert * FF
        gate_value = jnp.dot(normed, weight_in[0, :, start:start + FF], preferred_element_type=jnp.float32)
        up_value = jnp.dot(normed, weight_in[1, :, start:start + FF], preferred_element_type=jnp.float32)
        hidden = (jax.nn.silu(gate_value) * up_value).astype(jnp.bfloat16)
        hidden_blocks = hidden.reshape(count, blocks, UNITS).transpose(1, 0, 2).astype(jnp.float32)
        down_blocks = weight_out[start:start + FF].reshape(blocks, UNITS, D).astype(jnp.float32)
        pieces = jnp.einsum('gru,gud->grd', hidden_blocks, down_blocks)
        pieces = lax.optimization_barrier(pieces.astype(jnp.bfloat16)).astype(jnp.float32)
        expert_out = lax.optimization_barrier(jnp.sum(pieces, axis=0))
        weight = lax.optimization_barrier(jnp.sum(jnp.where(routes == expert, shares, jnp.zeros_like(shares)), axis=-1))
        total = total + weight[:, None] * expert_out
    return total.astype(jnp.bfloat16)

def reference(forward_in, reverse_in, norm_gain, gate_up_weight, down_weight, expert_ids, gate_weights):
    forward = forward_in
    reverse = reverse_in
    for moment in range(TICKS):

        def section_work(operands, moment=moment):
            fwd_rows, rev_rows, gain, weight_in, weight_out, routes, shares = operands
            rows_in = jnp.concatenate([fwd_rows, rev_rows], axis=0)
            chosen = jnp.concatenate([routes[moment, 0], routes[moment, 1]], axis=0)
            weights = jnp.concatenate([shares[moment, 0], shares[moment, 1]], axis=0)
            result = apply_layer(rows_in, gain, weight_in, weight_out, chosen, weights)
            return (result[:TOKENS], result[TOKENS:])
        new_forward, new_reverse = lax.map(section_work, (forward, reverse, norm_gain, gate_up_weight, down_weight, expert_ids, gate_weights))
        forward = jnp.roll(new_forward, 1, axis=0)
        reverse = jnp.roll(new_reverse, -1, axis=0)
    return (forward, reverse)
```

```python
import functools

import jax
import jax.numpy as jnp
from jax import lax
from jax.experimental import pallas as pl
from jax.experimental.pallas import tpu as pltpu
from jax.sharding import PartitionSpec as P

EXPERTS = 4
TICKS = 2
MOST = 6
WIDTH = 7168
HALF = WIDTH // 2
CHUNK = 512
STEPS = HALF // CHUNK
NX = NY = 4
PACK = 4 * MOST
BLOCK = NY * PACK
UNITS = 256
TOK = 16
MESH = pl.DeviceIdType.MESH


def kernel(
    fwd, rev, gain, wgu, wdn, mrow, mcol,
    outf, outr,
    rows, pk, xg, acc, ss, exg, exs, hid, wg, wd,
    rs1s, rs1r, rs2s, rs2r, yrs, yrr, zs, mrow2, mcol2, pick, pickt, mix,
    sem_row, sem_w, sem_m,
    row_s, row_r, w_s, w_r, m_s, m_r,
    yd_s, yd_r, xd_s, xd_r, xr_s, xr_r,
    ex_s, ex_r, hd_s, hd_r,
    r1_s, r1_r, r2_s, r2_r, yr_s, yr_r, z_s, z_r, zf_s, zf_r,
):
    s = lax.axis_index("section")
    me = lax.axis_index("expert")
    ns = lax.axis_size("section")
    c = lax.rem(me, 2)
    o = 1 - c
    x = lax.rem(me // 2, NX)
    y = me // (2 * NX)
    xp, xm, xo = lax.rem(x + 1, NX), lax.rem(x + NX - 1, NX), lax.rem(x + 2, NX)
    sp, sm = lax.rem(s + 1, ns), lax.rem(s + ns - 1, ns)

    def at(yy, xx, cc):
        return (s, (yy * NX + xx) * 2 + cc)

    partner = at(y, x, o)
    right, left = at(y, xp, c), at(y, xm, c)
    ups = [at(lax.rem(y + j, NY), x, c) for j in range(1, NY)]
    zdev = [[(sp, me - c + cc), (sm, me - c + cc)] for cc in range(2)]
    zsame = [(sp, me), (sm, me)]
    zother = [(sp, me - c + o), (sm, me - c + o)]

    def rcopy(src, dst, ssem, rsem, dev):
        return pltpu.make_async_remote_copy(
            src_ref=src, dst_ref=dst, send_sem=ssem, recv_sem=rsem,
            device_id=dev, device_id_type=MESH,
        )

    barrier = pltpu.get_barrier_semaphore()
    peers = [partner, right, left] + ups + zsame + zother
    for dev in peers:
        pl.semaphore_signal(barrier, inc=1, device_id=dev, device_id_type=MESH)
    pl.semaphore_wait(barrier, len(peers))

    def col(half, k):
        return pl.ds(pl.multiple_of(half * HALF + k * CHUNK, CHUNK), CHUNK)

    def row_copies(k):
        both = []
        for d, src in enumerate((fwd, rev)):
            both.append(pltpu.make_async_copy(
                src.at[:, col(c, k)], rows.at[0, k, 2 * d + c], sem_row.at[k, d]))
            both.append(rcopy(
                src.at[:, col(o, k)], rows.at[0, k, 2 * d + c], row_s.at[k, d], row_r.at[k, d], partner))
        return both

    def row_arrivals(k):
        return [
            rcopy(rows.at[0, k, 2 * d + o], rows.at[0, k, 2 * d + o], row_s.at[k, d], row_r.at[k, d], partner)
            for d in range(2)
        ]

    def weight_copies(k):
        made = []
        for g in range(2):
            made.append(pltpu.make_async_copy(
                wgu.at[g, col(c, k), :], wg.at[k, 2 * g + c], sem_w.at[k, g]))
            made.append(rcopy(
                wgu.at[g, col(o, k), :], wg.at[k, 2 * g + c], w_s.at[k, g], w_r.at[k, g], partner))
        made.append(pltpu.make_async_copy(wdn.at[:, col(c, k)], wd.at[k, c], sem_w.at[k, 2]))
        made.append(rcopy(wdn.at[:, col(o, k)], wd.at[k, c], w_s.at[k, 2], w_r.at[k, 2], partner))
        return made

    def weight_arrivals(k):
        return [
            rcopy(wg.at[k, 2 * g + o], wg.at[k, 2 * g + o], w_s.at[k, g], w_r.at[k, g], partner) for g in range(2)
        ] + [rcopy(wd.at[k, o], wd.at[k, o], w_s.at[k, 2], w_r.at[k, 2], partner)]

    tables = [
        rcopy(mrow, mrow2, m_s.at[0], m_r.at[0], partner),
        rcopy(mcol, mcol2, m_s.at[1], m_r.at[1], partner),
    ]
    for t in tables:
        t.start()

    @pl.loop(0, STEPS)
    def _(k):
        for cp in row_copies(k):
            cp.start()

    for t in tables:
        t.wait_recv()
    table_row = mrow[...] + mrow2[...]
    table_col = mcol[...] + mcol2[...]
    for t in range(TICKS):
        slot = lax.broadcasted_iota(jnp.int32, (4 * PACK, 4 * TOK), 0).astype(jnp.float32)
        pick[t] = jnp.where(slot == table_row[t:t + 1, :4 * TOK], 1.0, 0.0).astype(jnp.bfloat16)
        slot_t = lax.broadcasted_iota(jnp.int32, (4 * TOK, 4 * PACK), 1).astype(jnp.float32)
        pickt[t] = jnp.where(slot_t == table_col[:, 2 + t:3 + t], 1.0, 0.0).astype(jnp.bfloat16)
        mix[t] = jnp.broadcast_to(table_col[:, t:t + 1], (4 * TOK, 128))

    def yd(t, k, j):
        e = lax.rem(y + j, NY)
        return rcopy(pk.at[t, k, e], xg.at[t, k, x, y], yd_s.at[t, k, j - 1], yd_r.at[t, k, j - 1], ups[j - 1])

    def yd_in(t, k, j):
        spot = xg.at[t, k, x, lax.rem(y + NY - j, NY)]
        return rcopy(spot, spot, yd_s.at[t, k, j - 1], yd_r.at[t, k, j - 1], ups[j - 1])

    def z_next(t, k, d):
        return rcopy(
            zs.at[t, k, pl.ds(2 * d, 2)], rows.at[1, k, pl.ds(2 * d, 2)], z_s.at[k, d], z_r.at[k, d], zsame[d])

    def d0(t, k):
        if t == 0:
            for cp in row_copies(k):
                if not cp.is_remote:
                    cp.wait()
            for cp in row_arrivals(k):
                cp.wait_recv()
        else:
            for d in range(2):
                z_next(0, k, d).wait_recv()
        chunk = rows[t, k].reshape(4 * TOK, CHUNK)
        packed = jnp.dot(pick[t], chunk, preferred_element_type=jnp.float32)
        pk[t, k] = packed.reshape(NY, PACK, CHUNK).astype(jnp.bfloat16)
        for j in range(1, NY):
            yd(t, k, j).start()
        xg[t, k, x, y] = pk[t, k, y]

    def xd(t, k, way):
        spot = xg.at[t, k, x]
        return rcopy(spot, spot, xd_s.at[t, k, way], xd_r.at[t, k, way], (right, left)[way])

    def xd_in(t, k, way):
        spot = xg.at[t, k, (xm, xp)[way]]
        return rcopy(spot, spot, xd_s.at[t, k, way], xd_r.at[t, k, way], (right, left)[way])

    def d1(t, k):
        for j in range(1, NY):
            yd_in(t, k, j).wait_recv()
        for way in range(2):
            xd(t, k, way).start()

    def xr(t, k, way):
        spot = xg.at[t, k, (xm, xp)[way], pl.ds(2 * way, 2)]
        return rcopy(spot, spot, xr_s.at[t, k, way], xr_r.at[t, k, way], (right, left)[way])

    def xr_in(t, k, way):
        spot = xg.at[t, k, xo, pl.ds(2 * way, 2)]
        return rcopy(spot, spot, xr_s.at[t, k, way], xr_r.at[t, k, way], (right, left)[way])

    def d2(t, k):
        for way in range(2):
            xd_in(t, k, way).wait_recv()
            xr(t, k, way).start()

    def d3(t, k):
        for way in range(2):
            xr_in(t, k, way).wait_recv()
        if t == 0:
            for cp in weight_copies(k):
                if not cp.is_remote:
                    cp.wait()
            for cp in weight_arrivals(k):
                cp.wait_recv()
        held = xg[t, k].reshape(NX * BLOCK, CHUNK).astype(jnp.float32)
        square = held * held
        part = square[:, :128]
        for i in range(1, CHUNK // 128):
            part = part + square[:, 128 * i:128 * (i + 1)]
        scaled = (held * gain[c * STEPS + k]).astype(jnp.bfloat16)

        @pl.when(k == 0)
        def _():
            ss[t] = part.reshape(NX, BLOCK, 128)
            for q in range(4):
                acc[t, q] = jnp.dot(scaled, wg[k, q], preferred_element_type=jnp.float32).reshape(NX, BLOCK, UNITS)

        @pl.when(k > 0)
        def _():
            ss[t] += part.reshape(NX, BLOCK, 128)
            for q in range(4):
                acc[t, q] += jnp.dot(scaled, wg[k, q], preferred_element_type=jnp.float32).reshape(NX, BLOCK, UNITS)

    def ex(t, j):
        return [
            rcopy(acc.at[t, o, j], exg.at[t, 0, j], ex_s.at[t, 0, j], ex_r.at[t, 0, j], partner),
            rcopy(acc.at[t, 2 + o, j], exg.at[t, 1, j], ex_s.at[t, 1, j], ex_r.at[t, 1, j], partner),
            rcopy(ss.at[t, j], exs.at[t, j], ex_s.at[t, 2, j], ex_r.at[t, 2, j], partner),
        ]

    def hd(t, j):
        return rcopy(hid.at[t, c, j], hid.at[t, c, j], hd_s.at[t, j], hd_r.at[t, j], partner)

    def hd_in(t, j):
        return rcopy(hid.at[t, o, j], hid.at[t, o, j], hd_s.at[t, j], hd_r.at[t, j], partner)

    def middle(t):
        @pl.loop(0, NX)
        def _(i):
            for cp in ex(t, lax.rem(x + 2 + i, NX)):
                cp.start()

        @pl.loop(0, NX)
        def _(i):
            j = lax.rem(x + 2 + i, NX)
            for cp in ex(t, j):
                cp.wait_recv()
            total = jnp.sum(ss[t, j] + exs[t, j], axis=-1, keepdims=True)
            scale = lax.rsqrt(total * (1.0 / WIDTH) + 1e-06)
            gate = (acc[t, c, j] + exg[t, 0, j]) * scale
            up = (acc[t, 2 + c, j] + exg[t, 1, j]) * scale
            hid[t, c, j] = (gate / (1.0 + jnp.exp(-gate)) * up).astype(jnp.bfloat16)
            hd(t, j).start()

        @pl.loop(0, NX)
        def _(i):
            hd_in(t, lax.rem(x + 2 + i, NX)).wait_recv()

    def down(t, k, j):
        return jnp.dot(hid[t, 0, j], wd[k, 0], preferred_element_type=jnp.float32) + jnp.dot(
            hid[t, 1, j], wd[k, 1], preferred_element_type=jnp.float32)

    def r1(t, k, way):
        return rcopy(
            rs1s.at[t, k, way], rs1r.at[t, k, way], r1_s.at[t, k, way], r1_r.at[t, k, way], (right, left)[way])

    def r2(t, k, way):
        return rcopy(
            rs2s.at[t, k, way], rs2r.at[t, k, way], r2_s.at[t, k, way], r2_r.at[t, k, way], (right, left)[way])

    def c0(t, k):
        rs1s[t, k] = down(t, k, xo).reshape(2, BLOCK // 2, CHUNK).astype(jnp.bfloat16)
        for way in range(2):
            r1(t, k, way).start()

    def c1(t, k):
        for way in range(2):
            r1(t, k, way).wait_recv()
            part = down(t, k, (xp, xm)[way]).reshape(2, BLOCK // 2, CHUNK)
            got = rs1r[t, k, way].astype(jnp.float32)
            rs2s[t, k, way, way] = (part[way] + got).astype(jnp.bfloat16)
            rs2s[t, k, way, 1 - way] = part[1 - way].astype(jnp.bfloat16)
            r2(t, k, way).start()

    def yr(t, k, j):
        to = lax.rem(y + j, NY)
        return rcopy(yrs.at[t, k, to], yrr.at[t, k, y], yr_s.at[t, k, j - 1], yr_r.at[t, k, j - 1], ups[j - 1])

    def yr_in(t, k, j):
        spot = yrr.at[t, k, lax.rem(y + NY - j, NY)]
        return rcopy(spot, spot, yr_s.at[t, k, j - 1], yr_r.at[t, k, j - 1], ups[j - 1])

    def c2(t, k):
        for way in range(2):
            r2(t, k, way).wait_recv()
        full = down(t, k, x).reshape(2, BLOCK // 2, CHUNK)
        full = full + rs2r[t, k, 0].astype(jnp.float32) + rs2r[t, k, 1].astype(jnp.float32)
        yrs[t, k] = full.reshape(NY, PACK, CHUNK).astype(jnp.bfloat16)
        for j in range(1, NY):
            yr(t, k, j).start()
        yrr[t, k, y] = yrs[t, k, y]

    def z_last(k, d, cc):
        dst = (outf, outr)[d]
        return rcopy(zs.at[1, k, 2 * d + cc], dst.at[:, col(c, k)], zf_s.at[k, d, cc], zf_r.at[k, d, c], zdev[cc][d])

    def z_last_in(k, d, half):
        spot = (outf, outr)[d].at[:, col(half, k)]
        return rcopy(spot, spot, zf_s.at[k, d, half], zf_r.at[k, d, half], zsame[d])

    def c3(t, k):
        for j in range(1, NY):
            yr_in(t, k, j).wait_recv()
        back = yrr[t, k].astype(jnp.float32).reshape(4 * PACK, CHUNK).astype(jnp.bfloat16)
        mine = jnp.dot(pickt[t], back, preferred_element_type=jnp.float32)
        kept = rows[t, k].reshape(4 * TOK, CHUNK).astype(jnp.float32)
        made = kept + mix[t][:, :1] * mine
        zs[t, k] = made.reshape(4, TOK, CHUNK).astype(jnp.bfloat16)
        for d in range(2):
            if t == 0:
                z_next(0, k, d).start()
            else:
                for cc in range(2):
                    z_last(k, d, cc).start()

    def run(stages, steps):
        @pl.loop(0, steps)
        def _(i):
            for lag, f in stages:
                k = i - lag

                @pl.when((k >= 0) & (k < STEPS))
                def _():
                    f(k)

    def start_weights(k):
        for cp in weight_copies(k):
            cp.start()

    dispatch = [d0, d1, d2, d3]
    combine = [c0, c1, c2, c3]
    run([(0, functools.partial(d0, 0)), (0, start_weights), (1, functools.partial(d1, 0)),
         (2, functools.partial(d2, 0)), (3, functools.partial(d3, 0))], STEPS + 3)
    middle(0)
    run([(i, functools.partial(f, 0)) for i, f in enumerate(combine)]
        + [(4 + i, functools.partial(f, 1)) for i, f in enumerate(dispatch)], STEPS + 7)
    middle(1)
    run([(i, functools.partial(f, 1)) for i, f in enumerate(combine)], STEPS + 3)

    for t in tables:
        t.wait_send()

    @pl.loop(0, STEPS)
    def _(k):
        for d in range(2):
            for half in range(2):
                z_last_in(k, d, half).wait_recv()
                z_last(k, d, half).wait_send()
            z_next(0, k, d).wait_send()
        for cp in row_copies(k) + weight_copies(k):
            if cp.is_remote:
                cp.wait_send()
        for t in range(TICKS):
            for j in range(1, NY):
                yd(t, k, j).wait_send()
                yr(t, k, j).wait_send()
            for way in range(2):
                xd(t, k, way).wait_send()
                xr(t, k, way).wait_send()
                r1(t, k, way).wait_send()
                r2(t, k, way).wait_send()

    @pl.loop(0, NX)
    def _(j):
        for t in range(TICKS):
            for cp in ex(t, j):
                cp.wait_send()
            hd(t, j).wait_send()


def local(forward_in, reverse_in, norm_gain, gate_up_weight, down_weight, expert_ids, gate_weights):
    core = lax.rem(lax.axis_index("expert"), 2)
    ids = expert_ids[0, :, :, :, 0]
    earlier = jnp.arange(TOK)[None, :] < jnp.arange(TOK)[:, None]
    rank = jnp.sum((ids[:, :, :, None] == ids[:, :, None, :]) & earlier, axis=-1).astype(jnp.int32)
    way = jnp.arange(2, dtype=jnp.int32)[None, :, None]
    target = (ids * PACK + way * (2 * MOST) + core * MOST + rank).astype(jnp.float32)
    weight = gate_weights[0, :, :, :, 0]
    own = (jnp.arange(2) == core)[None, None, :, None]

    def spread(v):
        return jnp.where(own, v[:, :, None, :], 0.0).reshape(TICKS, 4 * TOK)

    target, weight = spread(target), spread(weight)
    table_row = jnp.pad(target, ((0, 8 - TICKS), (0, 128 - 4 * TOK)))
    table_col = jnp.pad(jnp.concatenate([weight, target], axis=0).T, ((0, 0), (0, 128 - 2 * TICKS)))
    gain = norm_gain[0].astype(jnp.float32).reshape(2 * STEPS, 1, CHUNK)

    bf, f32 = jnp.bfloat16, jnp.float32
    vmem = pltpu.VMEM
    dma = lambda *shape: pltpu.SemaphoreType.DMA(shape)
    anywhere = pl.BlockSpec(memory_space=pl.ANY)
    here = pl.BlockSpec(memory_space=pltpu.VMEM)
    T, K = TICKS, STEPS
    out = jax.ShapeDtypeStruct((TOK, WIDTH), bf)
    outs = pl.pallas_call(
        kernel,
        out_shape=(out, out),
        in_specs=[anywhere, anywhere, here, anywhere, anywhere, here, here],
        out_specs=(here, here),
        scratch_shapes=[
            vmem((T, K, 4, TOK, CHUNK), bf),
            vmem((T, K, NY, PACK, CHUNK), bf),
            vmem((T, K, NX, NY, PACK, CHUNK), bf),
            vmem((T, 4, NX, BLOCK, UNITS), f32),
            vmem((T, NX, BLOCK, 128), f32),
            vmem((T, 2, NX, BLOCK, UNITS), f32),
            vmem((T, NX, BLOCK, 128), f32),
            vmem((T, 2, NX, BLOCK, UNITS), bf),
            vmem((K, 4, CHUNK, UNITS), bf),
            vmem((K, 2, UNITS, CHUNK), bf),
            vmem((T, K, 2, BLOCK // 2, CHUNK), bf),
            vmem((T, K, 2, BLOCK // 2, CHUNK), bf),
            vmem((T, K, 2, 2, BLOCK // 2, CHUNK), bf),
            vmem((T, K, 2, 2, BLOCK // 2, CHUNK), bf),
            vmem((T, K, NY, PACK, CHUNK), bf),
            vmem((T, K, NY, PACK, CHUNK), bf),
            vmem((T, K, 4, TOK, CHUNK), bf),
            vmem((8, 128), f32),
            vmem((4 * TOK, 128), f32),
            vmem((T, 4 * PACK, 4 * TOK), bf),
            vmem((T, 4 * TOK, 4 * PACK), bf),
            vmem((T, 4 * TOK, 128), f32),
            dma(K, 2), dma(K, 3), dma(2),
            dma(K, 2), dma(K, 2), dma(K, 3), dma(K, 3), dma(2), dma(2),
            dma(T, K, 3), dma(T, K, 3), dma(T, K, 2), dma(T, K, 2), dma(T, K, 2), dma(T, K, 2),
            dma(T, 3, NX), dma(T, 3, NX), dma(T, NX), dma(T, NX),
            dma(T, K, 2), dma(T, K, 2), dma(T, K, 2), dma(T, K, 2),
            dma(T, K, 3), dma(T, K, 3), dma(K, 2), dma(K, 2), dma(K, 2, 2), dma(K, 2, 2),
        ],
        compiler_params=pltpu.CompilerParams(
            collective_id=0, has_side_effects=True, vmem_limit_bytes=60 * 2**20),
    )(forward_in[0], reverse_in[0], gain, gate_up_weight[0], down_weight[0], table_row, table_col)
    return tuple(v[None] for v in outs)


def solution(mesh):
    in_specs = (
        P("section", "expert", None),
        P("section", "expert", None),
        P("section", None),
        P("section", None, None, "expert"),
        P("section", "expert", None),
        P("section", None, None, "expert", None),
        P("section", None, None, "expert", None),
    )
    out_specs = (P("section", "expert", None), P("section", "expert", None))
    return jax.shard_map(local, mesh=mesh, in_specs=in_specs, out_specs=out_specs, check_vma=False)
```

```python
import functools

import jax
import jax.numpy as jnp
from jax import lax
from jax.experimental import pallas as pl
from jax.experimental.pallas import tpu as pltpu
from jax.sharding import PartitionSpec as P

EXPERTS = 4
TICKS = 2
MOST = 6
WIDTH = 7168
HALF = WIDTH // 2
CHUNK = 512
SUB = CHUNK // 2
STEPS = HALF // CHUNK
NX = NY = 4
PACK = 4 * MOST
BLOCK = NY * PACK
UNITS = 256
TOK = 16
ROWS = 4 * TOK
MESH = pl.DeviceIdType.MESH
LAG_FIRST, LAG_BOTH, LAG_LAST = (0, 2, 4), (0, 2, 4, 6, 8, 10), (0, 2, 4, 6)


def kernel(
    fwd, rev, gain_in, wgu, wdn, table,
    outf, outr,
    rows, nb, pk, yb, xi, acc, ss, exg, exs, hid, wg, wd,
    cs, cr, yrs, yrr, zs, zo, zl, zr, ls, la, lb, tab, pick, pickt, mix, gain,
    sem_row, sem_w,
    t_s, t_r, row_s, row_r, w_s, w_r,
    yd_s, yd_r, xd_s, xd_r, ex_s, ex_r, hd_s, hd_r,
    cx_s, cx_r, yr_s, yr_r, z_s, z_r, l_s, l_r,
):
    s = lax.axis_index("section")
    me = lax.axis_index("expert")
    ns = lax.axis_size("section")
    c = lax.rem(me, 2)
    o = 1 - c
    x = lax.rem(me // 2, NX)
    y = me // (2 * NX)
    xp, xm = lax.rem(x + 1, NX), lax.rem(x + NX - 1, NX)
    sz = (lax.rem(s + 1, ns), lax.rem(s + ns - 1, ns))
    f32, bf16 = jnp.float32, jnp.bfloat16

    def at(xx, cc, yy=y, zz=s):
        return (zz, (yy * NX + xx) * 2 + cc)

    partner = at(x, o)
    sides = (at(xp, c), at(xm, c))
    ups = [at(x, c, lax.rem(y + j, NY)) for j in range(1, NY)]

    def rcopy(src, dst, ssem, rsem, dev):
        return pltpu.make_async_remote_copy(
            src_ref=src, dst_ref=dst, send_sem=ssem, recv_sem=rsem, device_id=dev, device_id_type=MESH)

    def arrival(spot, ssem, rsem):
        return rcopy(spot, spot, ssem, rsem, partner)

    barrier = pltpu.get_barrier_semaphore()
    peers = [partner] + [at(xx, cc) for xx in (xp, xm) for cc in (c, o)] + ups
    peers += [at(xx, cc, y, zz) for zz in sz for xx in (x, xp, xm) for cc in (c, o)]
    for dev in peers:
        pl.semaphore_signal(barrier, inc=1, device_id=dev, device_id_type=MESH)
    pl.semaphore_wait(barrier, len(peers))

    def col(half, k):
        return pl.ds(pl.multiple_of(half * HALF + k * CHUNK, CHUNK), CHUNK)

    def sub(half, k, h):
        return pl.ds(pl.multiple_of(half * HALF + k * CHUNK + h * SUB, SUB), SUB)

    def table_sends():
        made = [rcopy(table, tab.at[0], t_s.at[0], t_r.at[0], partner)]
        for cc in range(2):
            made.append(rcopy(table, tab.at[1 + c], t_s.at[1 + cc], t_r.at[1 + c], at(xp, cc)))
            made.append(rcopy(table, tab.at[3 + c], t_s.at[3 + cc], t_r.at[3 + c], at(xm, cc)))
        return made

    def row_here(k, d):
        return pltpu.make_async_copy((fwd, rev)[d].at[:, col(c, k)], rows.at[0, k, 2 * d + c], sem_row.at[k, d])

    def row_sends(k, d):
        src = (fwd, rev)[d]
        made = [rcopy(src.at[:, col(o, k)], rows.at[0, k, 2 * d + c], row_s.at[k, d, 0], row_r.at[k, d, 0], partner)]
        for cc in range(2):
            made.append(rcopy(
                src.at[:, sub(cc, k, 0)], nb.at[0, k, 0, 2 * d + c], row_s.at[k, d, 1 + cc], row_r.at[k, d, 1 + c],
                at(xp, cc)))
            made.append(rcopy(
                src.at[:, sub(cc, k, 1)], nb.at[0, k, 1, 2 * d + c], row_s.at[k, d, 3 + cc], row_r.at[k, d, 3 + c],
                at(xm, cc)))
        return made

    def row_arrivals(k, d):
        made = [arrival(rows.at[0, k, 2 * d + o], row_s.at[k, d, 0], row_r.at[k, d, 0])]
        for h in range(2):
            for cc in range(2):
                made.append(arrival(
                    nb.at[0, k, h, 2 * d + cc], row_s.at[k, d, 1 + 2 * h + cc], row_r.at[k, d, 1 + 2 * h + cc]))
        return made

    def weights_here(k):
        made = [pltpu.make_async_copy(wgu.at[g, col(c, k), :], wg.at[k, 2 * g + c], sem_w.at[k, g]) for g in range(2)]
        return made + [pltpu.make_async_copy(wdn.at[:, col(c, k)], wd.at[k, c], sem_w.at[k, 2])]

    def weight_sends(k):
        made = [
            rcopy(wgu.at[g, col(o, k), :], wg.at[k, 2 * g + c], w_s.at[k, g], w_r.at[k, g], partner) for g in range(2)]
        return made + [rcopy(wdn.at[:, col(o, k)], wd.at[k, c], w_s.at[k, 2], w_r.at[k, 2], partner)]

    def weight_arrivals(k):
        made = [arrival(wg.at[k, 2 * g + o], w_s.at[k, g], w_r.at[k, g]) for g in range(2)]
        return made + [arrival(wd.at[k, o], w_s.at[k, 2], w_r.at[k, 2])]

    def start_weights(k):
        for cp in weights_here(k) + weight_sends(k):
            cp.start()

    for cp in table_sends():
        cp.start()

    @pl.loop(0, STEPS)
    def _(k):
        for d in range(2):
            for cp in [row_here(k, d)] + row_sends(k, d):
                cp.start()

    for i in range(2 * STEPS):
        gain[i] = gain_in[:, i * CHUNK:(i + 1) * CHUNK].astype(f32)
    for i in range(5):
        arrival(tab.at[i], t_s.at[i], t_r.at[i]).wait_recv()

    row_no = lax.broadcasted_iota(jnp.int32, (ROWS, ROWS), 0)
    col_no = lax.broadcasted_iota(jnp.int32, (ROWS, ROWS), 1)
    same = (row_no // TOK) == (col_no // TOK)
    base_row = (lax.broadcasted_iota(jnp.int32, (1, ROWS), 1) // TOK * MOST).astype(f32)
    base_col = (lax.broadcasted_iota(jnp.int32, (ROWS, 1), 0) // TOK * MOST).astype(f32)
    slot = lax.broadcasted_iota(jnp.int32, (BLOCK, ROWS), 0).astype(f32)
    slot_t = lax.broadcasted_iota(jnp.int32, (ROWS, BLOCK), 1).astype(f32)

    def upright(v):
        return jnp.sum(jnp.where(row_no == col_no, v, 0.0), axis=1, keepdims=True)

    for whose, full in enumerate((table[...] + tab[0], tab[1] + tab[2], tab[3] + tab[4])):
        for t in range(TICKS):
            ids, share = full[t:t + 1, :ROWS], full[TICKS + t:TICKS + t + 1, :ROWS]
            ids_col = upright(ids)
            equal = same & (ids == ids_col)
            rank_col = jnp.sum(jnp.where(equal & (col_no < row_no), 1.0, 0.0), axis=1, keepdims=True)
            rank_row = jnp.sum(jnp.where(equal & (row_no < col_no), 1.0, 0.0), axis=0, keepdims=True)
            pick[whose, t] = jnp.where(slot == ids * PACK + base_row + rank_row, 1.0, 0.0).astype(bf16)
            pickt[whose, t] = jnp.where(slot_t == ids_col * PACK + base_col + rank_col, 1.0, 0.0).astype(bf16)
            mix[whose, t] = jnp.broadcast_to(upright(share), (ROWS, 128))

    def yd(t, k, j):
        e = lax.rem(y + j, NY)
        return rcopy(pk.at[t, k, e], yb.at[t, k, y], yd_s.at[t, k, j - 1], yd_r.at[t, k, j - 1], ups[j - 1])

    def z_sends(k, d):
        spots = (zo.at[k, d], zl.at[k, d], zr.at[k, d])
        parts = (zs.at[k, d], zs.at[k, d, pl.ds(0, 2)], zs.at[k, d, pl.ds(2, 2)])
        return [
            rcopy(parts[i], spots[i], z_s.at[k, d, i], z_r.at[k, d, i], at((x, xp, xm)[i], c, y, sz[d]))
            for i in range(3)]

    def d0(t, k):
        if t == 0:
            for d in range(2):
                row_here(k, d).wait()
                for cp in row_arrivals(k, d):
                    cp.wait_recv()
            left, right = nb[0, k, 0].reshape(ROWS, SUB), nb[0, k, 1].reshape(ROWS, SUB)
        else:
            for d in range(2):
                for i, spot in enumerate((zo.at[k, d], zl.at[k, d], zr.at[k, d])):
                    arrival(spot, z_s.at[k, d, i], z_r.at[k, d, i]).wait_recv()

            def added(a, b):
                return (a.astype(f32) + b.astype(f32)).astype(bf16)

            rows[1, k, :, :, :SUB] = added(zo[k, :, 0], zr[k, :, 1]).reshape(4, TOK, SUB)
            rows[1, k, :, :, SUB:] = added(zo[k, :, 2], zl[k, :, 1]).reshape(4, TOK, SUB)
            left = added(zl[k, :, 0], zo[k, :, 3]).reshape(ROWS, SUB)
            right = added(zr[k, :, 0], zo[k, :, 1]).reshape(ROWS, SUB)

        def packed(whose, v):
            made = jnp.dot(pick[whose, t], v, preferred_element_type=f32)
            return made.reshape(NY, PACK, v.shape[1]).astype(bf16)

        own = packed(0, rows[t, k].reshape(ROWS, CHUNK))
        pk[t, k, :, 0, 0] = packed(1, left)
        pk[t, k, :, 0, 1] = own[:, :, SUB:]
        pk[t, k, :, 1, 0] = own[:, :, :SUB]
        pk[t, k, :, 1, 1] = packed(2, right)
        for j in range(1, NY):
            yd(t, k, j).start()
        yb[t, k, y] = pk[t, k, y]

    def xd(t, k, way):
        return rcopy(yb.at[t, k, :, way], xi.at[t, k, way], xd_s.at[t, k, way], xd_r.at[t, k, way], sides[way])

    def d1(t, k):
        for j in range(1, NY):
            arrival(yb.at[t, k, lax.rem(y + NY - j, NY)], yd_s.at[t, k, j - 1], yd_r.at[t, k, j - 1]).wait_recv()
        for way in range(2):
            xd(t, k, way).start()

    def d2(t, k):
        for way in range(2):
            xd(t, k, way).wait_recv()
        if t == 0:
            for cp in weights_here(k):
                cp.wait()
            for cp in weight_arrivals(k):
                cp.wait_recv()

        def block(ref, way, h):
            v = ref[t, k, :, way, h] if ref is yb else ref[t, k, way, :, h]
            return v.astype(f32).reshape(BLOCK, SUB)

        first = jnp.concatenate([block(yb, 1, 0), block(xi, 1, 0), block(xi, 0, 0), block(yb, 0, 0)], axis=0)
        second = jnp.concatenate([block(yb, 0, 1), block(yb, 1, 1), block(xi, 1, 1), block(xi, 0, 1)], axis=0)
        held = jnp.concatenate([first, second], axis=1)
        square = held * held
        part = square[:, :128]
        for i in range(1, CHUNK // 128):
            part = part + square[:, 128 * i:128 * (i + 1)]
        scaled = (held * gain[c * STEPS + k]).astype(bf16)

        @pl.when(k == 0)
        def _():
            ss[t] = part.reshape(NX, BLOCK, 128)
            for q in range(4):
                acc[t, q] = jnp.dot(scaled, wg[k, q], preferred_element_type=f32).reshape(NX, BLOCK, UNITS)

        @pl.when(k > 0)
        def _():
            ss[t] += part.reshape(NX, BLOCK, 128)
            for q in range(4):
                acc[t, q] += jnp.dot(scaled, wg[k, q], preferred_element_type=f32).reshape(NX, BLOCK, UNITS)

    def ex(t, j):
        return [
            rcopy(acc.at[t, o, j], exg.at[t, 0, j], ex_s.at[t, 0, j], ex_r.at[t, 0, j], partner),
            rcopy(acc.at[t, 2 + o, j], exg.at[t, 1, j], ex_s.at[t, 1, j], ex_r.at[t, 1, j], partner),
            rcopy(ss.at[t, j], exs.at[t, j], ex_s.at[t, 2, j], ex_r.at[t, 2, j], partner),
        ]

    def hd(t, j):
        return rcopy(hid.at[t, c, j], hid.at[t, c, j], hd_s.at[t, j], hd_r.at[t, j], partner)

    def middle(t):
        for j in range(NX):
            for cp in ex(t, j):
                cp.start()

        @pl.loop(0, NX)
        def _(j):
            for cp in ex(t, j):
                cp.wait_recv()
            total = jnp.sum(ss[t, j] + exs[t, j], axis=-1, keepdims=True)
            scale = lax.rsqrt(total * (1.0 / WIDTH) + 1e-06)
            gate = (acc[t, c, j] + exg[t, 0, j]) * scale
            up = (acc[t, 2 + c, j] + exg[t, 1, j]) * scale
            hid[t, c, j] = (gate / (1.0 + jnp.exp(-gate)) * up).astype(bf16)
            hd(t, j).start()

        for j in range(NX):
            arrival(hid.at[t, o, j], hd_s.at[t, j], hd_r.at[t, j]).wait_recv()

    def down(t, k, j, h):
        return jnp.dot(hid[t, 0, j], wd[k, 0, :, h * SUB:(h + 1) * SUB], preferred_element_type=f32) + jnp.dot(
            hid[t, 1, j], wd[k, 1, :, h * SUB:(h + 1) * SUB], preferred_element_type=f32)

    def cx(t, k, way):
        return rcopy(cs.at[t, k, way], cr.at[t, k, way], cx_s.at[t, k, way], cx_r.at[t, k, way], sides[way])

    def c0(t, k):
        for way in range(2):
            for h in range(2):
                cs[t, k, way, h] = down(t, k, 1 + way + h, h).astype(bf16)
            cx(t, k, way).start()

    def yr(t, k, j):
        to = lax.rem(y + j, NY)
        return rcopy(yrs.at[t, k, to], yrr.at[t, k, y], yr_s.at[t, k, j - 1], yr_r.at[t, k, j - 1], ups[j - 1])

    def c1(t, k):
        for way in range(2):
            cx(t, k, way).wait_recv()
        for p in range(2):
            for h in range(2):
                j = 0 if p == 0 else (3, 1)[h]
                total = down(t, k, j, h) + cr[t, k, p ^ h, h].astype(f32)
                yrs[t, k, :, p, h] = total.reshape(NY, PACK, SUB).astype(bf16)
        for j in range(1, NY):
            yr(t, k, j).start()
        yrr[t, k, y] = yrs[t, k, y]

    def last_sends(k, d):
        made = []
        for cc in range(2):
            spot = ls.at[k, d, cc]
            made.append(rcopy(
                spot.at[pl.ds(0, 2)], la.at[k, d, c], l_s.at[k, d, cc, 0], l_r.at[k, d, c, 0], at(x, cc, y, sz[d])))
            made.append(rcopy(
                spot.at[2], lb.at[k, d, c, 0], l_s.at[k, d, cc, 1], l_r.at[k, d, c, 1], at(xm, cc, y, sz[d])))
            made.append(rcopy(
                spot.at[3], lb.at[k, d, c, 1], l_s.at[k, d, cc, 2], l_r.at[k, d, c, 2], at(xp, cc, y, sz[d])))
        return made

    def c2(t, k):
        for j in range(1, NY):
            arrival(yrr.at[t, k, lax.rem(y + NY - j, NY)], yr_s.at[t, k, j - 1], yr_r.at[t, k, j - 1]).wait_recv()

        def mine(whose, p, h):
            back = yrr[t, k, :, p, h].astype(f32).reshape(BLOCK, SUB).astype(bf16)
            return mix[whose, t][:, :1] * jnp.dot(pickt[whose, t], back, preferred_element_type=f32)

        kept = rows[t, k].reshape(ROWS, CHUNK).astype(f32)
        own = [(kept[:, h * SUB:(h + 1) * SUB] + mine(0, 0, h)).astype(bf16) for h in range(2)]
        left, right = mine(1, 1, 0).astype(bf16), mine(2, 1, 1).astype(bf16)
        if t == 0:
            for i, v in enumerate((own[0], right, own[1], left)):
                zs[k, :, i] = v.reshape(2, 2, TOK, SUB)
        else:
            for i, v in enumerate((own[0], own[1], left, right)):
                ls[k, :, :, i] = v.reshape(2, 2, TOK, SUB)
        for d in range(2):
            for cp in z_sends(k, d) if t == 0 else last_sends(k, d):
                cp.start()

    def finish(k):
        for d, out in enumerate((outf, outr)):
            for half in range(2):
                arrival(la.at[k, d, half], l_s.at[k, d, half, 0], l_r.at[k, d, half, 0]).wait_recv()
                for h in range(2):
                    arrival(lb.at[k, d, half, h], l_s.at[k, d, half, 1 + h], l_r.at[k, d, half, 1 + h]).wait_recv()
                for h in range(2):
                    out[:, sub(half, k, h)] = (
                        la[k, d, half, h].astype(f32) + lb[k, d, half, h].astype(f32)).astype(bf16)

    def run(stages):
        @pl.loop(0, STEPS + max(lag for lag, _ in stages))
        def _(i):
            for lag, f in stages:
                k = i - lag

                @pl.when((k >= 0) & (k < STEPS))
                def _():
                    f(k)

    def bound(t, *fs):
        return [functools.partial(f, t) for f in fs]

    run([(0, start_weights)] + list(zip(LAG_FIRST, bound(0, d0, d1, d2))))
    middle(0)
    run(list(zip(LAG_BOTH, bound(0, c0, c1, c2) + bound(1, d0, d1, d2))))
    middle(1)
    run(list(zip(LAG_LAST, bound(1, c0, c1, c2) + [finish])))

    for cp in table_sends():
        cp.wait_send()

    @pl.loop(0, STEPS)
    def _(k):
        for d in range(2):
            for cp in row_sends(k, d) + z_sends(k, d) + last_sends(k, d):
                cp.wait_send()
        for cp in weight_sends(k):
            cp.wait_send()
        for t in range(TICKS):
            for j in range(1, NY):
                yd(t, k, j).wait_send()
                yr(t, k, j).wait_send()
            for way in range(2):
                xd(t, k, way).wait_send()
                cx(t, k, way).wait_send()

    @pl.loop(0, NX)
    def _(j):
        for t in range(TICKS):
            for cp in ex(t, j):
                cp.wait_send()
            hd(t, j).wait_send()


def local(forward_in, reverse_in, norm_gain, gate_up_weight, down_weight, expert_ids, gate_weights):
    core = lax.rem(lax.axis_index("expert"), 2)
    f32, bf = jnp.float32, jnp.bfloat16
    both = jnp.concatenate([expert_ids.astype(f32), gate_weights], axis=0).reshape(2 * TICKS, 2, 1, TOK)
    own = (jnp.arange(2) == core)[None, None, :, None]
    table = jnp.where(own, both, 0.0).reshape(2 * TICKS, ROWS)
    table = jnp.pad(table, ((0, 8 - 2 * TICKS), (0, 128 - ROWS)))

    vmem = pltpu.VMEM
    dma = lambda *shape: pltpu.SemaphoreType.DMA(shape)
    anywhere = pl.BlockSpec(memory_space=pl.ANY)
    here = pl.BlockSpec(memory_space=pltpu.VMEM)
    T, K = TICKS, STEPS
    out = jax.ShapeDtypeStruct((TOK, WIDTH), bf)
    outs = pl.pallas_call(
        kernel,
        out_shape=(out, out),
        in_specs=[anywhere, anywhere, here, anywhere, anywhere, here],
        out_specs=(here, here),
        scratch_shapes=[
            vmem((T, K, 4, TOK, CHUNK), bf),
            vmem((1, K, 2, 4, TOK, SUB), bf),
            vmem((T, K, NY, 2, 2, PACK, SUB), bf),
            vmem((T, K, NY, 2, 2, PACK, SUB), bf),
            vmem((T, K, 2, NY, 2, PACK, SUB), bf),
            vmem((T, 4, NX, BLOCK, UNITS), f32),
            vmem((T, NX, BLOCK, 128), f32),
            vmem((T, 2, NX, BLOCK, UNITS), f32),
            vmem((T, NX, BLOCK, 128), f32),
            vmem((T, 2, NX, BLOCK, UNITS), bf),
            vmem((K, 4, CHUNK, UNITS), bf),
            vmem((K, 2, UNITS, CHUNK), bf),
            vmem((T, K, 2, 2, BLOCK, SUB), bf),
            vmem((T, K, 2, 2, BLOCK, SUB), bf),
            vmem((T, K, NY, 2, 2, PACK, SUB), bf),
            vmem((T, K, NY, 2, 2, PACK, SUB), bf),
            vmem((K, 2, 4, 2, TOK, SUB), bf),
            vmem((K, 2, 4, 2, TOK, SUB), bf),
            vmem((K, 2, 2, 2, TOK, SUB), bf),
            vmem((K, 2, 2, 2, TOK, SUB), bf),
            vmem((K, 2, 2, 4, TOK, SUB), bf),
            vmem((K, 2, 2, 2, TOK, SUB), bf),
            vmem((K, 2, 2, 2, TOK, SUB), bf),
            vmem((5, 8, 128), f32),
            vmem((3, T, BLOCK, ROWS), bf),
            vmem((3, T, ROWS, BLOCK), bf),
            vmem((3, T, ROWS, 128), f32),
            vmem((2 * K, 1, CHUNK), f32),
            dma(K, 2), dma(K, 3),
            dma(5), dma(5), dma(K, 2, 5), dma(K, 2, 5), dma(K, 3), dma(K, 3),
            dma(T, K, 3), dma(T, K, 3), dma(T, K, 2), dma(T, K, 2),
            dma(T, 3, NX), dma(T, 3, NX), dma(T, NX), dma(T, NX),
            dma(T, K, 2), dma(T, K, 2), dma(T, K, 3), dma(T, K, 3),
            dma(K, 2, 3), dma(K, 2, 3), dma(K, 2, 2, 3), dma(K, 2, 2, 3),
        ],
        compiler_params=pltpu.CompilerParams(
            collective_id=0, has_side_effects=True, vmem_limit_bytes=60 * 2**20),
    )(forward_in[0], reverse_in[0], norm_gain, gate_up_weight[0], down_weight[0], table)
    return tuple(v[None] for v in outs)


def solution(mesh):
    in_specs = (
        P("section", "expert", None),
        P("section", "expert", None),
        P("section", None),
        P("section", None, None, "expert"),
        P("section", "expert", None),
        P("section", None, None, "expert", None),
        P("section", None, None, "expert", None),
    )
    out_specs = (P("section", "expert", None), P("section", "expert", None))
    return jax.shard_map(local, mesh=mesh, in_specs=in_specs, out_specs=out_specs, check_vma=False)
```

```python
import functools

import jax
import jax.numpy as jnp
from jax import lax
from jax.experimental import pallas as pl
from jax.experimental.pallas import tpu as pltpu
from jax.sharding import PartitionSpec as P

EXPERTS = 4
TICKS = 2
MOST = 6
WIDTH = 7168
HALF = WIDTH // 2
CHUNK = 512
SUB = CHUNK // 2
STEPS = HALF // CHUNK
NX = NY = 4
SLOTS = 2 * MOST
PACK = 2 * SLOTS
BLOCK = NY * SLOTS
PACKS = NY * PACK
UNITS = 256
TOK = 16
ROWS = 2 * TOK
MESH = pl.DeviceIdType.MESH
LAGS = ((9, 5, 2, 1, 3, 4, 3), (3, 4, 2, 1, 5, 9, 7))
BEHIND = 7
ORDER = (2, 3, 4, 8, 0, 1, 9, 5, 6, 7)


def kernel(
    fwd, rev, gain_in, wgu, wdn, ids_in, share_in,
    outf, outr,
    rows, nb, pk, yb, xi, acc, ss, exg, exs, hid, wg, wd,
    cs, cr, yrs, yrr, zs, zo, zl, zr, ls, la, lb, tab, pick, pickt, mix, gain, apart, join, table,
    sem_row, sem_w,
    t_s, t_r, row_s, row_r, w_s, w_r,
    yd_s, yd_r, xd_s, xd_r, ex_s, ex_r, hd_s, hd_r,
    cx_s, cx_r, yr_s, yr_r, z_s, z_r, l_s, l_r,
):
    s = lax.axis_index("section")
    me = lax.axis_index("expert")
    ns = lax.axis_size("section")
    c = lax.rem(me, 2)
    o = 1 - c
    x = lax.rem(me // 2, NX)
    y = me // (2 * NX)
    xp, xm = lax.rem(x + 1, NX), lax.rem(x + NX - 1, NX)
    sz = (lax.rem(s + 1, ns), lax.rem(s + ns - 1, ns))
    f32, bf16 = jnp.float32, jnp.bfloat16

    def at(xx, cc, yy=y, zz=s):
        return (zz, (yy * NX + xx) * 2 + cc)

    partner = at(x, o)
    sides = (at(xp, c), at(xm, c))
    ups = [at(x, c, lax.rem(y + j, NY)) for j in range(1, NY)]

    def rcopy(src, dst, ssem, rsem, dev):
        return pltpu.make_async_remote_copy(
            src_ref=src, dst_ref=dst, send_sem=ssem, recv_sem=rsem, device_id=dev, device_id_type=MESH)

    def arrival(spot, ssem, rsem):
        return rcopy(spot, spot, ssem, rsem, partner)

    barrier = pltpu.get_barrier_semaphore()
    peers = [partner] + [at(xx, cc) for xx in (xp, xm) for cc in (c, o)] + ups
    peers += [at(xx, cc, y, zz) for zz in sz for xx in (x, xp, xm) for cc in (c, o)]
    for dev in peers:
        pl.semaphore_signal(barrier, inc=1, device_id=dev, device_id_type=MESH)

    for i in range(2 * STEPS):
        gain[i] = gain_in[:, i * CHUNK:(i + 1) * CHUNK].astype(f32)

    def number(shape, axis):
        return lax.broadcasted_iota(jnp.int32, shape, axis).astype(f32)

    lanes = lax.broadcasted_iota(jnp.int32, (TOK, 128), 1)
    token = lax.broadcasted_iota(jnp.int32, (TOK, 128), 0)
    group = lanes // TOK
    placed = (lanes - group * TOK == token) & ((group == c) | (group == 2 + c))
    listed = [ids_in[i].astype(f32) for i in range(4)] + [share_in[i] for i in range(4)]
    table[...] = jnp.dot(
        jnp.concatenate(listed, axis=0), jnp.where(placed, 1.0, 0.0), precision=lax.Precision.HIGHEST,
        preferred_element_type=f32)

    whole = jnp.floor((number((NX * BLOCK, 1), 0) + 0.5) * (1.0 / SLOTS))
    place = number((NX * BLOCK, 1), 0) + SLOTS * whole
    for h in range(2):
        apart[h] = jnp.where(number((NX * BLOCK, NX * PACKS), 1) == place + h * SLOTS, 1.0, 0.0).astype(bf16)
    whole = jnp.floor((number((PACKS, 1), 0) + 0.5) * (1.0 / PACK))
    inside = number((PACKS, 1), 0) - PACK * whole
    place = SLOTS * whole + inside + jnp.where(inside < SLOTS, 0.0, BLOCK - SLOTS)
    join[...] = jnp.where(number((PACKS, PACKS), 1) == place, 1.0, 0.0).astype(bf16)

    pl.semaphore_wait(barrier, len(peers))

    def col(half, k):
        return pl.ds(pl.multiple_of(half * HALF + k * CHUNK, CHUNK), CHUNK)

    def sub(half, k, h):
        return pl.ds(pl.multiple_of(half * HALF + k * CHUNK + h * SUB, SUB), SUB)

    def table_sends():
        made = [rcopy(table, tab.at[0], t_s.at[0], t_r.at[0], partner)]
        for cc in range(2):
            made.append(rcopy(table, tab.at[1 + c], t_s.at[1 + cc], t_r.at[1 + c], at(xp, cc)))
            made.append(rcopy(table, tab.at[3 + c], t_s.at[3 + cc], t_r.at[3 + c], at(xm, cc)))
        return made

    def row_here(d, k):
        return pltpu.make_async_copy((fwd, rev)[d].at[:, col(c, k)], rows.at[d, 0, k, c], sem_row.at[d, k])

    def row_sends(d, k):
        src = (fwd, rev)[d]
        made = [rcopy(src.at[:, col(o, k)], rows.at[d, 0, k, c], row_s.at[d, k, 0], row_r.at[d, k, 0], partner)]
        for cc in range(2):
            made.append(rcopy(
                src.at[:, sub(cc, k, 0)], nb.at[d, k, 0, c], row_s.at[d, k, 1 + cc], row_r.at[d, k, 1 + c], at(xp, cc)))
            made.append(rcopy(
                src.at[:, sub(cc, k, 1)], nb.at[d, k, 1, c], row_s.at[d, k, 3 + cc], row_r.at[d, k, 3 + c], at(xm, cc)))
        return made

    def row_arrivals(d, k):
        made = [arrival(rows.at[d, 0, k, o], row_s.at[d, k, 0], row_r.at[d, k, 0])]
        for h in range(2):
            for cc in range(2):
                i = 1 + 2 * h + cc
                made.append(arrival(nb.at[d, k, h, cc], row_s.at[d, k, i], row_r.at[d, k, i]))
        return made

    def weights_here(k):
        made = [pltpu.make_async_copy(wgu.at[g, col(c, k), :], wg.at[k, 2 * g + c], sem_w.at[k, g]) for g in range(2)]
        return made + [pltpu.make_async_copy(wdn.at[:, col(c, k)], wd.at[k, c], sem_w.at[k, 2])]

    def weight_sends(k):
        made = [
            rcopy(wgu.at[g, col(o, k), :], wg.at[k, 2 * g + c], w_s.at[k, g], w_r.at[k, g], partner) for g in range(2)]
        return made + [rcopy(wdn.at[:, col(o, k)], wd.at[k, c], w_s.at[k, 2], w_r.at[k, 2], partner)]

    def weight_arrivals(k):
        made = [arrival(wg.at[k, 2 * g + o], w_s.at[k, g], w_r.at[k, g]) for g in range(2)]
        return made + [arrival(wd.at[k, o], w_s.at[k, 2], w_r.at[k, 2])]

    def start_weights(k):
        for cp in weights_here(k) + weight_sends(k):
            cp.start()

    for cp in table_sends():
        cp.start()
    for d in range(2):

        @pl.loop(0, STEPS)
        def _(k):
            for cp in [row_here(d, k)] + row_sends(d, k):
                cp.start()

    for i in range(5):
        arrival(tab.at[i], t_s.at[i], t_r.at[i]).wait_recv()

    twice = 2 * ROWS
    row_no = lax.broadcasted_iota(jnp.int32, (twice, twice), 0)
    col_no = lax.broadcasted_iota(jnp.int32, (twice, twice), 1)
    same = (row_no // TOK) == (col_no // TOK)
    lane = lax.broadcasted_iota(jnp.int32, (1, twice), 1)
    line = lax.broadcasted_iota(jnp.int32, (twice, 1), 0)
    slot, slot_t = number((PACKS, twice), 0), number((twice, PACKS), 1)

    def core_of(v):
        return jnp.where((v // TOK == 1) | (v // TOK == 3), float(MOST), 0.0)

    def upright(v):
        return jnp.sum(jnp.where(row_no == col_no, v, 0.0), axis=1, keepdims=True)

    def onehot(v):
        return jnp.where(v, 1.0, 0.0).astype(bf16)

    full = (table[...] + tab[0], tab[1] + tab[2], tab[3] + tab[4])
    for d in range(2):
        for t in range(TICKS):
            found = []
            for one in full:
                ids = one[2 * t + d:2 * t + d + 1, :twice]
                share = upright(one[4 + 2 * t + d:5 + 2 * t + d, :twice])
                ids_col = upright(ids)
                equal = same & (ids == ids_col)
                rank_col = jnp.sum(jnp.where(equal & (col_no < row_no), 1.0, 0.0), axis=1, keepdims=True)
                rank_row = jnp.sum(jnp.where(equal & (row_no < col_no), 1.0, 0.0), axis=0, keepdims=True)
                found.append((
                    ids * PACK + core_of(lane) + rank_row, ids_col * PACK + core_of(line) + rank_col, share))
            own, left, right = found
            pick[d, t, 0] = onehot(slot == jnp.where(lane < ROWS, left[0], own[0] + SLOTS))
            pick[d, t, 1] = onehot(slot == jnp.where(lane < ROWS, own[0], right[0] + SLOTS))
            pickt[d, t, 0] = onehot(slot_t == jnp.where(line < ROWS, own[1], own[1] + SLOTS))
            pickt[d, t, 1] = onehot(slot_t == jnp.where(line < ROWS, left[1], right[1] + SLOTS))
            mix[d, t, 0] = jnp.broadcast_to(own[2], (twice, 128))
            mix[d, t, 1] = jnp.broadcast_to(jnp.where(line < ROWS, left[2], right[2]), (twice, 128))

    def yd(d, t, k, j):
        e = lax.rem(y + j, NY)
        return rcopy(
            pk.at[d, t, k, e], yb.at[d, t, k, y], yd_s.at[d, t, k, j - 1], yd_r.at[d, t, k, j - 1], ups[j - 1])

    def z_sends(d, k):
        spots = (zo.at[d, k], zl.at[d, k], zr.at[d, k])
        parts = (zs.at[d, k], zs.at[d, k, pl.ds(0, 2)], zs.at[d, k, pl.ds(2, 2)])
        return [
            rcopy(parts[i], spots[i], z_s.at[d, k, i], z_r.at[d, k, i], at((x, xp, xm)[i], c, y, sz[d]))
            for i in range(3)]

    def d0(d, t, k):
        if t == 0:
            row_here(d, k).wait()
            for cp in row_arrivals(d, k):
                cp.wait_recv()
            left, right = nb[d, k, 0].reshape(ROWS, SUB), nb[d, k, 1].reshape(ROWS, SUB)
        else:
            for i, spot in enumerate((zo.at[d, k], zl.at[d, k], zr.at[d, k])):
                arrival(spot, z_s.at[d, k, i], z_r.at[d, k, i]).wait_recv()

            def added(a, b):
                return (a.astype(f32) + b.astype(f32)).astype(bf16)

            rows[d, 1, k, :, :, :SUB] = added(zo[d, k, 0], zr[d, k, 1])
            rows[d, 1, k, :, :, SUB:] = added(zo[d, k, 2], zl[d, k, 1])
            left = added(zl[d, k, 0], zo[d, k, 3]).reshape(ROWS, SUB)
            right = added(zr[d, k, 0], zo[d, k, 1]).reshape(ROWS, SUB)
        own = rows[d, t, k].reshape(ROWS, CHUNK)
        for way, pair in enumerate(((left, own[:, SUB:]), (own[:, :SUB], right))):
            made = jnp.dot(pick[d, t, way], jnp.concatenate(pair, axis=0), preferred_element_type=f32)
            pk[d, t, k, :, way] = made.reshape(NY, PACK, SUB).astype(bf16)
        for j in range(1, NY):
            yd(d, t, k, j).start()
        yb[d, t, k, y] = pk[d, t, k, y]

    def xd(d, t, k, way):
        return rcopy(
            yb.at[d, t, k, :, way], xi.at[d, t, k, way], xd_s.at[d, t, k, way], xd_r.at[d, t, k, way], sides[way])

    def d1(d, t, k):
        for j in range(1, NY):
            spot = yb.at[d, t, k, lax.rem(y + NY - j, NY)]
            arrival(spot, yd_s.at[d, t, k, j - 1], yd_r.at[d, t, k, j - 1]).wait_recv()
        for way in range(2):
            xd(d, t, k, way).start()

    def d2(d, t, k):
        for way in range(2):
            xd(d, t, k, way).wait_recv()
        if d == 0 and t == 0:
            for cp in weights_here(k):
                cp.wait()
            for cp in weight_arrivals(k):
                cp.wait_recv()

        def flat(v):
            return v.astype(f32).reshape(PACKS, SUB).astype(bf16)

        mine = [flat(yb[d, t, k, :, way]) for way in range(2)]
        theirs = [flat(xi[d, t, k, way]) for way in range(2)]
        first = jnp.concatenate([mine[1], theirs[1], theirs[0], mine[0]], axis=0)
        second = jnp.concatenate([mine[0], mine[1], theirs[1], theirs[0]], axis=0)
        held = jnp.concatenate([
            jnp.dot(apart[0], first, preferred_element_type=f32),
            jnp.dot(apart[1], second, preferred_element_type=f32)], axis=1)
        square = held * held
        part = square[:, :128]
        for i in range(1, CHUNK // 128):
            part = part + square[:, 128 * i:128 * (i + 1)]
        scaled = (held * gain[c * STEPS + k]).astype(bf16)

        @pl.when(k == 0)
        def _():
            ss[d, t] = part.reshape(NX, BLOCK, 128)
            for q in range(4):
                acc[d, t, q] = jnp.dot(scaled, wg[k, q], preferred_element_type=f32).reshape(NX, BLOCK, UNITS)

        @pl.when(k > 0)
        def _():
            ss[d, t] += part.reshape(NX, BLOCK, 128)
            for q in range(4):
                acc[d, t, q] += jnp.dot(scaled, wg[k, q], preferred_element_type=f32).reshape(NX, BLOCK, UNITS)

    def ex(d, t):
        return [
            rcopy(acc.at[d, t, o], exg.at[d, t, 0], ex_s.at[d, t, 0], ex_r.at[d, t, 0], partner),
            rcopy(acc.at[d, t, 2 + o], exg.at[d, t, 1], ex_s.at[d, t, 1], ex_r.at[d, t, 1], partner),
            rcopy(ss.at[d, t], exs.at[d, t], ex_s.at[d, t, 2], ex_r.at[d, t, 2], partner),
        ]

    def hd(d, t):
        return rcopy(hid.at[d, t, c], hid.at[d, t, c], hd_s.at[d, t], hd_r.at[d, t], partner)

    def m0(d, t, k):
        for cp in ex(d, t):
            cp.start()

    def m1(d, t, k):
        for cp in ex(d, t):
            cp.wait_recv()

        @pl.loop(0, NX)
        def _(j):
            total = jnp.sum(ss[d, t, j] + exs[d, t, j], axis=-1, keepdims=True)
            scale = lax.rsqrt(total * (1.0 / WIDTH) + 1e-06)
            gate = (acc[d, t, c, j] + exg[d, t, 0, j]) * scale
            up = (acc[d, t, 2 + c, j] + exg[d, t, 1, j]) * scale
            hid[d, t, c, j] = (gate / (1.0 + jnp.exp(-gate)) * up).astype(bf16)

        hd(d, t).start()

    def m2(d, t, k):
        arrival(hid.at[d, t, o], hd_s.at[d, t], hd_r.at[d, t]).wait_recv()

    def down(d, t, k, js, h):
        total = None
        for cc in range(2):
            units = jnp.concatenate([hid[d, t, cc, j] for j in js], axis=0)
            made = jnp.dot(units, wd[k, cc, :, h * SUB:(h + 1) * SUB], preferred_element_type=f32)
            total = made if total is None else total + made
        return [total[i * BLOCK:(i + 1) * BLOCK] for i in range(len(js))]

    def cx(d, t, k, way):
        return rcopy(
            cs.at[d, t, k, way], cr.at[d, t, k, way], cx_s.at[d, t, k, way], cx_r.at[d, t, k, way], sides[way])

    def c0(d, t, k):
        for h in range(2):
            for way, v in enumerate(down(d, t, k, (1 + h, 2 + h), h)):
                cs[d, t, k, way, h] = v.astype(bf16)
        for way in range(2):
            cx(d, t, k, way).start()

    def yr(d, t, k, j):
        to = lax.rem(y + j, NY)
        return rcopy(
            yrs.at[d, t, k, to], yrr.at[d, t, k, y], yr_s.at[d, t, k, j - 1], yr_r.at[d, t, k, j - 1], ups[j - 1])

    def c1(d, t, k):
        for way in range(2):
            cx(d, t, k, way).wait_recv()
        both = [[], []]
        for h in range(2):
            for p, v in enumerate(down(d, t, k, (0, (3, 1)[h]), h)):
                both[p].append((v + cr[d, t, k, p ^ h, h].astype(f32)).astype(bf16))
        for p in range(2):
            made = jnp.dot(join[...], jnp.concatenate(both[p], axis=0), preferred_element_type=f32)
            yrs[d, t, k, :, p] = made.reshape(NY, PACK, SUB).astype(bf16)
        for j in range(1, NY):
            yr(d, t, k, j).start()
        yrr[d, t, k, y] = yrs[d, t, k, y]

    def last_sends(d, k):
        made = []
        for cc in range(2):
            spot = ls.at[d, k, cc]
            made.append(rcopy(
                spot.at[pl.ds(0, 2)], la.at[d, k, c], l_s.at[d, k, cc, 0], l_r.at[d, k, c, 0], at(x, cc, y, sz[d])))
            made.append(rcopy(
                spot.at[2], lb.at[d, k, c, 0], l_s.at[d, k, cc, 1], l_r.at[d, k, c, 1], at(xm, cc, y, sz[d])))
            made.append(rcopy(
                spot.at[3], lb.at[d, k, c, 1], l_s.at[d, k, cc, 2], l_r.at[d, k, c, 2], at(xp, cc, y, sz[d])))
        return made

    def c2(d, t, k):
        for j in range(1, NY):
            spot = yrr.at[d, t, k, lax.rem(y + NY - j, NY)]
            arrival(spot, yr_s.at[d, t, k, j - 1], yr_r.at[d, t, k, j - 1]).wait_recv()
        parts = []
        for p in range(2):
            back = yrr[d, t, k, :, p].astype(f32).reshape(PACKS, SUB).astype(bf16)
            got = mix[d, t, p][:, :1] * jnp.dot(pickt[d, t, p], back, preferred_element_type=f32)
            parts.append([got[h * ROWS:(h + 1) * ROWS] for h in range(2)])
        kept = rows[d, t, k].reshape(ROWS, CHUNK).astype(f32)
        own = [(kept[:, h * SUB:(h + 1) * SUB] + parts[0][h]).astype(bf16) for h in range(2)]
        left, right = parts[1][0].astype(bf16), parts[1][1].astype(bf16)
        if t == 0:
            for i, v in enumerate((own[0], right, own[1], left)):
                zs[d, k, i] = v.reshape(2, TOK, SUB)
        else:
            for i, v in enumerate((own[0], own[1], left, right)):
                ls[d, k, :, i] = v.reshape(2, TOK, SUB)
        for cp in z_sends(d, k) if t == 0 else last_sends(d, k):
            cp.start()

    def finish(d, t, k):
        out = (outf, outr)[d]
        for half in range(2):
            arrival(la.at[d, k, half], l_s.at[d, k, half, 0], l_r.at[d, k, half, 0]).wait_recv()
            for h in range(2):
                arrival(lb.at[d, k, half, h], l_s.at[d, k, half, 1 + h], l_r.at[d, k, half, 1 + h]).wait_recv()
            for h in range(2):
                out[:, sub(half, k, h)] = (la[d, k, half, h].astype(f32) + lb[d, k, half, h].astype(f32)).astype(bf16)

    starts = {}
    begin = 0
    for t in range(TICKS):
        x_send, gate_up, swap, hidden, x_sum, mixing, after = LAGS[t]
        starts[t, 0], starts[t, 1], starts[t, 2] = begin, begin + x_send, begin + x_send + gate_up
        starts[t, 3] = starts[t, 2] + STEPS - 1
        starts[t, 4] = starts[t, 3] + swap
        starts[t, 5] = starts[t, 6] = starts[t, 4] + hidden
        starts[t, 7] = starts[t, 6] + x_sum
        starts[t, 8] = starts[t, 7] + mixing
        begin = starts[t, 8] + after
    starts[TICKS - 1, 9] = begin
    stages = ((d0, STEPS), (d1, STEPS), (d2, STEPS), (m0, 1), (m1, 1), (m2, 1), (c0, STEPS), (c1, STEPS), (c2, STEPS),
              (finish, STEPS))

    @pl.loop(0, begin + STEPS + BEHIND)
    def _(i):
        @pl.when(i < STEPS)
        def _():
            start_weights(i)

        for stage in ORDER:
            f, count = stages[stage]
            for t in reversed(range(TICKS)):
                for d in range(2):
                    if (t, stage) in starts:
                        k = i - starts[t, stage] - d * BEHIND

                        @pl.when((k >= 0) & (k < count))
                        def _():
                            f(d, t, k)

    for cp in table_sends():
        cp.wait_send()
    for d in range(2):

        @pl.loop(0, STEPS)
        def _(k):
            for cp in row_sends(d, k) + z_sends(d, k) + last_sends(d, k):
                cp.wait_send()
            for t in range(TICKS):
                for j in range(1, NY):
                    yd(d, t, k, j).wait_send()
                    yr(d, t, k, j).wait_send()
                for way in range(2):
                    xd(d, t, k, way).wait_send()
                    cx(d, t, k, way).wait_send()

        for t in range(TICKS):
            for cp in ex(d, t):
                cp.wait_send()
            hd(d, t).wait_send()

    @pl.loop(0, STEPS)
    def _(k):
        for cp in weight_sends(k):
            cp.wait_send()


def local(forward_in, reverse_in, norm_gain, gate_up_weight, down_weight, expert_ids, gate_weights):
    f32, bf = jnp.float32, jnp.bfloat16
    vmem = pltpu.VMEM
    dma = lambda *shape: pltpu.SemaphoreType.DMA(shape)
    anywhere = pl.BlockSpec(memory_space=pl.ANY)
    here = pl.BlockSpec(memory_space=pltpu.VMEM)
    S, T, K = 2, TICKS, STEPS
    out = jax.ShapeDtypeStruct((TOK, WIDTH), bf)
    outs = pl.pallas_call(
        kernel,
        out_shape=(out, out),
        in_specs=[anywhere, anywhere, here, anywhere, anywhere, here, here],
        out_specs=(here, here),
        scratch_shapes=[
            vmem((S, T, K, 2, TOK, CHUNK), bf),
            vmem((S, K, 2, 2, TOK, SUB), bf),
            vmem((S, T, K, NY, 2, PACK, SUB), bf),
            vmem((S, T, K, NY, 2, PACK, SUB), bf),
            vmem((S, T, K, 2, NY, PACK, SUB), bf),
            vmem((S, T, 4, NX, BLOCK, UNITS), f32),
            vmem((S, T, NX, BLOCK, 128), f32),
            vmem((S, T, 2, NX, BLOCK, UNITS), f32),
            vmem((S, T, NX, BLOCK, 128), f32),
            vmem((S, T, 2, NX, BLOCK, UNITS), bf),
            vmem((K, 4, CHUNK, UNITS), bf),
            vmem((K, 2, UNITS, CHUNK), bf),
            vmem((S, T, K, 2, 2, BLOCK, SUB), bf),
            vmem((S, T, K, 2, 2, BLOCK, SUB), bf),
            vmem((S, T, K, NY, 2, PACK, SUB), bf),
            vmem((S, T, K, NY, 2, PACK, SUB), bf),
            vmem((S, K, 4, 2, TOK, SUB), bf),
            vmem((S, K, 4, 2, TOK, SUB), bf),
            vmem((S, K, 2, 2, TOK, SUB), bf),
            vmem((S, K, 2, 2, TOK, SUB), bf),
            vmem((S, K, 2, 4, TOK, SUB), bf),
            vmem((S, K, 2, 2, TOK, SUB), bf),
            vmem((S, K, 2, 2, TOK, SUB), bf),
            vmem((5, 8, 128), f32),
            vmem((S, T, 2, PACKS, 2 * ROWS), bf),
            vmem((S, T, 2, 2 * ROWS, PACKS), bf),
            vmem((S, T, 2, 2 * ROWS, 128), f32),
            vmem((2 * K, 1, CHUNK), f32),
            vmem((2, NX * BLOCK, NX * PACKS), bf),
            vmem((PACKS, PACKS), bf),
            vmem((8, 128), f32),
            dma(S, K), dma(K, 3),
            dma(5), dma(5), dma(S, K, 5), dma(S, K, 5), dma(K, 3), dma(K, 3),
            dma(S, T, K, 3), dma(S, T, K, 3), dma(S, T, K, 2), dma(S, T, K, 2),
            dma(S, T, 3), dma(S, T, 3), dma(S, T), dma(S, T),
            dma(S, T, K, 2), dma(S, T, K, 2), dma(S, T, K, 3), dma(S, T, K, 3),
            dma(S, K, 3), dma(S, K, 3), dma(S, K, 2, 3), dma(S, K, 2, 3),
        ],
        compiler_params=pltpu.CompilerParams(
            collective_id=0, has_side_effects=True, vmem_limit_bytes=50 * 2**20),
    )(forward_in[0], reverse_in[0], norm_gain, gate_up_weight[0], down_weight[0],
      expert_ids.reshape(2 * TICKS, 1, TOK), gate_weights.reshape(2 * TICKS, 1, TOK))
    return tuple(v[None] for v in outs)


def solution(mesh):
    in_specs = (
        P("section", "expert", None),
        P("section", "expert", None),
        P("section", None),
        P("section", None, None, "expert"),
        P("section", "expert", None),
        P("section", None, None, "expert", None),
        P("section", None, None, "expert", None),
    )
    out_specs = (P("section", "expert", None), P("section", "expert", None))
    return jax.shard_map(local, mesh=mesh, in_specs=in_specs, out_specs=out_specs, check_vma=False)
```

```python
import functools

import jax
import jax.numpy as jnp
from jax import lax
from jax.experimental import pallas as pl
from jax.experimental.pallas import tpu as pltpu
from jax.sharding import PartitionSpec as P

EXPERTS = 4
TICKS = 2
MOST = 6
WIDTH = 7168
HALF = WIDTH // 2
CHUNK = 512
SUB = CHUNK // 2
STEPS = HALF // CHUNK
NX = NY = 4
PACK = 4 * MOST
BLOCK = NY * PACK
UNITS = 256
TOK = 16
ROWS = 4 * TOK
MESH = pl.DeviceIdType.MESH
LAG_FIRST, LAG_BOTH, LAG_LAST = (0, 3, 6), (0, 2, 4, 6, 8, 10), (0, 3, 6, 9)


def kernel(
    fwd, rev, gain_in, wgu, wdn, ids_in, share_in,
    outf, outr,
    rows, nb, pk, yb, xi, acc, ss, exg, exs, hid, wg, wd,
    cs, cr, yrs, yrr, zs, zo, zl, zr, ls, la, lb, tab, pick, pickt, mix, gain, table,
    sem_row, sem_w,
    t_s, t_r, row_s, row_r, w_s, w_r,
    yd_s, yd_r, xd_s, xd_r, ex_s, ex_r, hd_s, hd_r,
    cx_s, cx_r, yr_s, yr_r, z_s, z_r, l_s, l_r,
):
    s = lax.axis_index("section")
    me = lax.axis_index("expert")
    ns = lax.axis_size("section")
    c = lax.rem(me, 2)
    o = 1 - c
    x = lax.rem(me // 2, NX)
    y = me // (2 * NX)
    xp, xm = lax.rem(x + 1, NX), lax.rem(x + NX - 1, NX)
    sz = (lax.rem(s + 1, ns), lax.rem(s + ns - 1, ns))
    f32, bf16 = jnp.float32, jnp.bfloat16

    def at(xx, cc, yy=y, zz=s):
        return (zz, (yy * NX + xx) * 2 + cc)

    partner = at(x, o)
    sides = (at(xp, c), at(xm, c))
    ups = [at(x, c, lax.rem(y + j, NY)) for j in range(1, NY)]

    def rcopy(src, dst, ssem, rsem, dev):
        return pltpu.make_async_remote_copy(
            src_ref=src, dst_ref=dst, send_sem=ssem, recv_sem=rsem, device_id=dev, device_id_type=MESH)

    def arrival(spot, ssem, rsem):
        return rcopy(spot, spot, ssem, rsem, partner)

    barrier = pltpu.get_barrier_semaphore()
    peers = [partner] + [at(xx, cc) for xx in (xp, xm) for cc in (c, o)] + ups
    peers += [at(xx, cc, y, zz) for zz in sz for xx in (x, xp, xm) for cc in (c, o)]
    for dev in peers:
        pl.semaphore_signal(barrier, inc=1, device_id=dev, device_id_type=MESH)

    for i in range(2 * STEPS):
        gain[i] = gain_in[:, i * CHUNK:(i + 1) * CHUNK].astype(f32)

    lanes = lax.broadcasted_iota(jnp.int32, (TOK, 128), 1)
    token = lax.broadcasted_iota(jnp.int32, (TOK, 128), 0)
    group = lanes // TOK
    filled = None
    for d in range(2):
        listed = [ids_in[2 * t + d].astype(f32) for t in range(TICKS)] + [share_in[2 * t + d] for t in range(TICKS)]
        placed = (lanes - group * TOK == token) & (group == 2 * d + c)
        part = jnp.dot(
            jnp.concatenate(listed + listed, axis=0), jnp.where(placed, 1.0, 0.0), precision=lax.Precision.HIGHEST,
            preferred_element_type=f32)
        filled = part if filled is None else filled + part
    table[...] = filled

    pl.semaphore_wait(barrier, len(peers))

    def col(half, k):
        return pl.ds(pl.multiple_of(half * HALF + k * CHUNK, CHUNK), CHUNK)

    def sub(half, k, h):
        return pl.ds(pl.multiple_of(half * HALF + k * CHUNK + h * SUB, SUB), SUB)

    def table_sends():
        made = [rcopy(table, tab.at[0], t_s.at[0], t_r.at[0], partner)]
        for cc in range(2):
            made.append(rcopy(table, tab.at[1 + c], t_s.at[1 + cc], t_r.at[1 + c], at(xp, cc)))
            made.append(rcopy(table, tab.at[3 + c], t_s.at[3 + cc], t_r.at[3 + c], at(xm, cc)))
        return made

    def row_here(k, d):
        return pltpu.make_async_copy((fwd, rev)[d].at[:, col(c, k)], rows.at[0, k, 2 * d + c], sem_row.at[k, d])

    def row_sends(k, d):
        src = (fwd, rev)[d]
        made = [rcopy(src.at[:, col(o, k)], rows.at[0, k, 2 * d + c], row_s.at[k, d, 0], row_r.at[k, d, 0], partner)]
        for cc in range(2):
            made.append(rcopy(
                src.at[:, sub(cc, k, 0)], nb.at[0, k, 0, 2 * d + c], row_s.at[k, d, 1 + cc], row_r.at[k, d, 1 + c],
                at(xp, cc)))
            made.append(rcopy(
                src.at[:, sub(cc, k, 1)], nb.at[0, k, 1, 2 * d + c], row_s.at[k, d, 3 + cc], row_r.at[k, d, 3 + c],
                at(xm, cc)))
        return made

    def row_arrivals(k, d):
        made = [arrival(rows.at[0, k, 2 * d + o], row_s.at[k, d, 0], row_r.at[k, d, 0])]
        for h in range(2):
            for cc in range(2):
                made.append(arrival(
                    nb.at[0, k, h, 2 * d + cc], row_s.at[k, d, 1 + 2 * h + cc], row_r.at[k, d, 1 + 2 * h + cc]))
        return made

    def weights_here(k):
        made = [pltpu.make_async_copy(wgu.at[g, col(c, k), :], wg.at[k, 2 * g + c], sem_w.at[k, g]) for g in range(2)]
        return made + [pltpu.make_async_copy(wdn.at[:, col(c, k)], wd.at[k, c], sem_w.at[k, 2])]

    def weight_sends(k):
        made = [
            rcopy(wgu.at[g, col(o, k), :], wg.at[k, 2 * g + c], w_s.at[k, g], w_r.at[k, g], partner) for g in range(2)]
        return made + [rcopy(wdn.at[:, col(o, k)], wd.at[k, c], w_s.at[k, 2], w_r.at[k, 2], partner)]

    def weight_arrivals(k):
        made = [arrival(wg.at[k, 2 * g + o], w_s.at[k, g], w_r.at[k, g]) for g in range(2)]
        return made + [arrival(wd.at[k, o], w_s.at[k, 2], w_r.at[k, 2])]

    def start_weights(k):
        for cp in weights_here(k) + weight_sends(k):
            cp.start()

    for cp in table_sends():
        cp.start()

    @pl.loop(0, STEPS)
    def _(k):
        for d in range(2):
            for cp in [row_here(k, d)] + row_sends(k, d):
                cp.start()

    for i in range(5):
        arrival(tab.at[i], t_s.at[i], t_r.at[i]).wait_recv()

    row_no = lax.broadcasted_iota(jnp.int32, (ROWS, ROWS), 0)
    col_no = lax.broadcasted_iota(jnp.int32, (ROWS, ROWS), 1)
    same = (row_no // TOK) == (col_no // TOK)
    base_row = (lax.broadcasted_iota(jnp.int32, (1, ROWS), 1) // TOK * MOST).astype(f32)
    base_col = (lax.broadcasted_iota(jnp.int32, (ROWS, 1), 0) // TOK * MOST).astype(f32)
    slot = lax.broadcasted_iota(jnp.int32, (BLOCK, ROWS), 0).astype(f32)
    slot_t = lax.broadcasted_iota(jnp.int32, (ROWS, BLOCK), 1).astype(f32)

    def upright(v):
        return jnp.sum(jnp.where(row_no == col_no, v, 0.0), axis=1, keepdims=True)

    for whose, full in enumerate((table[...] + tab[0], tab[1] + tab[2], tab[3] + tab[4])):
        for t in range(TICKS):
            ids, share = full[t:t + 1, :ROWS], full[TICKS + t:TICKS + t + 1, :ROWS]
            ids_col = upright(ids)
            equal = same & (ids == ids_col)
            rank_col = jnp.sum(jnp.where(equal & (col_no < row_no), 1.0, 0.0), axis=1, keepdims=True)
            rank_row = jnp.sum(jnp.where(equal & (row_no < col_no), 1.0, 0.0), axis=0, keepdims=True)
            pick[whose, t] = jnp.where(slot == ids * PACK + base_row + rank_row, 1.0, 0.0).astype(bf16)
            pickt[whose, t] = jnp.where(slot_t == ids_col * PACK + base_col + rank_col, 1.0, 0.0).astype(bf16)
            mix[whose, t] = jnp.broadcast_to(upright(share), (ROWS, 128))

    def yd(t, k, j):
        e = lax.rem(y + j, NY)
        return rcopy(pk.at[t, k, e], yb.at[t, k, y], yd_s.at[t, k, j - 1], yd_r.at[t, k, j - 1], ups[j - 1])

    def z_sends(k, d):
        spots = (zo.at[k, d], zl.at[k, d], zr.at[k, d])
        parts = (zs.at[k, d], zs.at[k, d, pl.ds(0, 2)], zs.at[k, d, pl.ds(2, 2)])
        return [
            rcopy(parts[i], spots[i], z_s.at[k, d, i], z_r.at[k, d, i], at((x, xp, xm)[i], c, y, sz[d]))
            for i in range(3)]

    def d0(t, k):
        if t == 0:
            for d in range(2):
                row_here(k, d).wait()
                for cp in row_arrivals(k, d):
                    cp.wait_recv()
            left, right = nb[0, k, 0].reshape(ROWS, SUB), nb[0, k, 1].reshape(ROWS, SUB)
        else:
            for d in range(2):
                for i, spot in enumerate((zo.at[k, d], zl.at[k, d], zr.at[k, d])):
                    arrival(spot, z_s.at[k, d, i], z_r.at[k, d, i]).wait_recv()

            def added(a, b):
                return (a.astype(f32) + b.astype(f32)).astype(bf16)

            rows[1, k, :, :, :SUB] = added(zo[k, :, 0], zr[k, :, 1]).reshape(4, TOK, SUB)
            rows[1, k, :, :, SUB:] = added(zo[k, :, 2], zl[k, :, 1]).reshape(4, TOK, SUB)
            left = added(zl[k, :, 0], zo[k, :, 3]).reshape(ROWS, SUB)
            right = added(zr[k, :, 0], zo[k, :, 1]).reshape(ROWS, SUB)

        def packed(whose, v):
            made = jnp.dot(pick[whose, t], v, preferred_element_type=f32)
            return made.reshape(NY, PACK, v.shape[1]).astype(bf16)

        own = packed(0, rows[t, k].reshape(ROWS, CHUNK))
        pk[t, k, :, 0, 0] = packed(1, left)
        pk[t, k, :, 0, 1] = own[:, :, SUB:]
        pk[t, k, :, 1, 0] = own[:, :, :SUB]
        pk[t, k, :, 1, 1] = packed(2, right)
        for j in range(1, NY):
            yd(t, k, j).start()
        yb[t, k, y] = pk[t, k, y]

    def xd(t, k, way):
        return rcopy(yb.at[t, k, :, way], xi.at[t, k, way], xd_s.at[t, k, way], xd_r.at[t, k, way], sides[way])

    def d1(t, k):
        for j in range(1, NY):
            arrival(yb.at[t, k, lax.rem(y + NY - j, NY)], yd_s.at[t, k, j - 1], yd_r.at[t, k, j - 1]).wait_recv()
        for way in range(2):
            xd(t, k, way).start()

    def d2(t, k):
        for way in range(2):
            xd(t, k, way).wait_recv()
        if t == 0:
            for cp in weights_here(k):
                cp.wait()
            for cp in weight_arrivals(k):
                cp.wait_recv()

        def block(ref, way, h):
            v = ref[t, k, :, way, h] if ref is yb else ref[t, k, way, :, h]
            return v.astype(f32).reshape(BLOCK, SUB)

        first = jnp.concatenate([block(yb, 1, 0), block(xi, 1, 0), block(xi, 0, 0), block(yb, 0, 0)], axis=0)
        second = jnp.concatenate([block(yb, 0, 1), block(yb, 1, 1), block(xi, 1, 1), block(xi, 0, 1)], axis=0)
        held = jnp.concatenate([first, second], axis=1)
        square = held * held
        part = square[:, :128]
        for i in range(1, CHUNK // 128):
            part = part + square[:, 128 * i:128 * (i + 1)]
        scaled = (held * gain[c * STEPS + k]).astype(bf16)

        @pl.when(k == 0)
        def _():
            ss[t] = part.reshape(NX, BLOCK, 128)
            for q in range(4):
                acc[t, q] = jnp.dot(scaled, wg[k, q], preferred_element_type=f32).reshape(NX, BLOCK, UNITS)

        @pl.when(k > 0)
        def _():
            ss[t] += part.reshape(NX, BLOCK, 128)
            for q in range(4):
                acc[t, q] += jnp.dot(scaled, wg[k, q], preferred_element_type=f32).reshape(NX, BLOCK, UNITS)

    def ex(t, j):
        return [
            rcopy(acc.at[t, o, j], exg.at[t, 0, j], ex_s.at[t, 0, j], ex_r.at[t, 0, j], partner),
            rcopy(acc.at[t, 2 + o, j], exg.at[t, 1, j], ex_s.at[t, 1, j], ex_r.at[t, 1, j], partner),
            rcopy(ss.at[t, j], exs.at[t, j], ex_s.at[t, 2, j], ex_r.at[t, 2, j], partner),
        ]

    def hd(t, j):
        return rcopy(hid.at[t, c, j], hid.at[t, c, j], hd_s.at[t, j], hd_r.at[t, j], partner)

    def middle(t):
        for j in (1, 2, 3, 0):
            for cp in ex(t, j):
                cp.start()

        @pl.loop(0, NX)
        def _(i):
            j = lax.rem(i + 1, NX)
            for cp in ex(t, j):
                cp.wait_recv()
            total = jnp.sum(ss[t, j] + exs[t, j], axis=-1, keepdims=True)
            scale = lax.rsqrt(total * (1.0 / WIDTH) + 1e-06)
            gate = (acc[t, c, j] + exg[t, 0, j]) * scale
            up = (acc[t, 2 + c, j] + exg[t, 1, j]) * scale
            hid[t, c, j] = (gate / (1.0 + jnp.exp(-gate)) * up).astype(bf16)
            hd(t, j).start()

        for j in range(1, NX):
            arrival(hid.at[t, o, j], hd_s.at[t, j], hd_r.at[t, j]).wait_recv()

    def down(t, k, j, h):
        return jnp.dot(hid[t, 0, j], wd[k, 0, :, h * SUB:(h + 1) * SUB], preferred_element_type=f32) + jnp.dot(
            hid[t, 1, j], wd[k, 1, :, h * SUB:(h + 1) * SUB], preferred_element_type=f32)

    def cx(t, k, way):
        return rcopy(cs.at[t, k, way], cr.at[t, k, way], cx_s.at[t, k, way], cx_r.at[t, k, way], sides[way])

    def c0(t, k):
        for way in range(2):
            for h in range(2):
                cs[t, k, way, h] = down(t, k, 1 + way + h, h).astype(bf16)
            cx(t, k, way).start()

    def yr(t, k, j):
        to = lax.rem(y + j, NY)
        return rcopy(yrs.at[t, k, to], yrr.at[t, k, y], yr_s.at[t, k, j - 1], yr_r.at[t, k, j - 1], ups[j - 1])

    def c1(t, k):
        @pl.when(k == 0)
        def _():
            arrival(hid.at[t, o, 0], hd_s.at[t, 0], hd_r.at[t, 0]).wait_recv()

        for way in range(2):
            cx(t, k, way).wait_recv()
        for p in range(2):
            for h in range(2):
                j = 0 if p == 0 else (3, 1)[h]
                total = down(t, k, j, h) + cr[t, k, p ^ h, h].astype(f32)
                yrs[t, k, :, p, h] = total.reshape(NY, PACK, SUB).astype(bf16)
        for j in range(1, NY):
            yr(t, k, j).start()
        yrr[t, k, y] = yrs[t, k, y]

    def last_sends(k, d):
        made = []
        for cc in range(2):
            spot = ls.at[k, d, cc]
            made.append(rcopy(
                spot.at[pl.ds(0, 2)], la.at[k, d, c], l_s.at[k, d, cc, 0], l_r.at[k, d, c, 0], at(x, cc, y, sz[d])))
            made.append(rcopy(
                spot.at[2], lb.at[k, d, c, 0], l_s.at[k, d, cc, 1], l_r.at[k, d, c, 1], at(xm, cc, y, sz[d])))
            made.append(rcopy(
                spot.at[3], lb.at[k, d, c, 1], l_s.at[k, d, cc, 2], l_r.at[k, d, c, 2], at(xp, cc, y, sz[d])))
        return made

    def c2(t, k):
        for j in range(1, NY):
            arrival(yrr.at[t, k, lax.rem(y + NY - j, NY)], yr_s.at[t, k, j - 1], yr_r.at[t, k, j - 1]).wait_recv()

        def mine(whose, p, h):
            back = yrr[t, k, :, p, h].astype(f32).reshape(BLOCK, SUB).astype(bf16)
            return mix[whose, t][:, :1] * jnp.dot(pickt[whose, t], back, preferred_element_type=f32)

        kept = rows[t, k].reshape(ROWS, CHUNK).astype(f32)
        own = [(kept[:, h * SUB:(h + 1) * SUB] + mine(0, 0, h)).astype(bf16) for h in range(2)]
        left, right = mine(1, 1, 0).astype(bf16), mine(2, 1, 1).astype(bf16)
        if t == 0:
            for i, v in enumerate((own[0], right, own[1], left)):
                zs[k, :, i] = v.reshape(2, 2, TOK, SUB)
        else:
            for i, v in enumerate((own[0], own[1], left, right)):
                ls[k, :, :, i] = v.reshape(2, 2, TOK, SUB)
        for d in range(2):
            for cp in z_sends(k, d) if t == 0 else last_sends(k, d):
                cp.start()

    def finish(k):
        for d, out in enumerate((outf, outr)):
            for half in range(2):
                arrival(la.at[k, d, half], l_s.at[k, d, half, 0], l_r.at[k, d, half, 0]).wait_recv()
                for h in range(2):
                    arrival(lb.at[k, d, half, h], l_s.at[k, d, half, 1 + h], l_r.at[k, d, half, 1 + h]).wait_recv()
                for h in range(2):
                    out[:, sub(half, k, h)] = (
                        la[k, d, half, h].astype(f32) + lb[k, d, half, h].astype(f32)).astype(bf16)

    def run(stages):
        @pl.loop(0, STEPS + max(lag for lag, _ in stages))
        def _(i):
            for lag, f in stages:
                k = i - lag

                @pl.when((k >= 0) & (k < STEPS))
                def _():
                    f(k)

    def bound(t, *fs):
        return [functools.partial(f, t) for f in fs]

    run([(0, start_weights)] + list(zip(LAG_FIRST, bound(0, d0, d1, d2))))
    middle(0)
    run(list(zip(LAG_BOTH, bound(0, c0, c1, c2) + bound(1, d0, d1, d2))))
    middle(1)
    run(list(zip(LAG_LAST, bound(1, c0, c1, c2) + [finish])))

    for cp in table_sends():
        cp.wait_send()

    @pl.loop(0, STEPS)
    def _(k):
        for d in range(2):
            for cp in row_sends(k, d) + z_sends(k, d) + last_sends(k, d):
                cp.wait_send()
        for cp in weight_sends(k):
            cp.wait_send()
        for t in range(TICKS):
            for j in range(1, NY):
                yd(t, k, j).wait_send()
                yr(t, k, j).wait_send()
            for way in range(2):
                xd(t, k, way).wait_send()
                cx(t, k, way).wait_send()

    @pl.loop(0, NX)
    def _(j):
        for t in range(TICKS):
            for cp in ex(t, j):
                cp.wait_send()
            hd(t, j).wait_send()


def local(forward_in, reverse_in, norm_gain, gate_up_weight, down_weight, expert_ids, gate_weights):
    f32, bf = jnp.float32, jnp.bfloat16
    vmem = pltpu.VMEM
    dma = lambda *shape: pltpu.SemaphoreType.DMA(shape)
    anywhere = pl.BlockSpec(memory_space=pl.ANY)
    here = pl.BlockSpec(memory_space=pltpu.VMEM)
    T, K = TICKS, STEPS
    out = jax.ShapeDtypeStruct((TOK, WIDTH), bf)
    outs = pl.pallas_call(
        kernel,
        out_shape=(out, out),
        in_specs=[anywhere, anywhere, here, anywhere, anywhere, here, here],
        out_specs=(here, here),
        scratch_shapes=[
            vmem((T, K, 4, TOK, CHUNK), bf),
            vmem((1, K, 2, 4, TOK, SUB), bf),
            vmem((T, K, NY, 2, 2, PACK, SUB), bf),
            vmem((T, K, NY, 2, 2, PACK, SUB), bf),
            vmem((T, K, 2, NY, 2, PACK, SUB), bf),
            vmem((T, 4, NX, BLOCK, UNITS), f32),
            vmem((T, NX, BLOCK, 128), f32),
            vmem((T, 2, NX, BLOCK, UNITS), f32),
            vmem((T, NX, BLOCK, 128), f32),
            vmem((T, 2, NX, BLOCK, UNITS), bf),
            vmem((K, 4, CHUNK, UNITS), bf),
            vmem((K, 2, UNITS, CHUNK), bf),
            vmem((T, K, 2, 2, BLOCK, SUB), bf),
            vmem((T, K, 2, 2, BLOCK, SUB), bf),
            vmem((T, K, NY, 2, 2, PACK, SUB), bf),
            vmem((T, K, NY, 2, 2, PACK, SUB), bf),
            vmem((K, 2, 4, 2, TOK, SUB), bf),
            vmem((K, 2, 4, 2, TOK, SUB), bf),
            vmem((K, 2, 2, 2, TOK, SUB), bf),
            vmem((K, 2, 2, 2, TOK, SUB), bf),
            vmem((K, 2, 2, 4, TOK, SUB), bf),
            vmem((K, 2, 2, 2, TOK, SUB), bf),
            vmem((K, 2, 2, 2, TOK, SUB), bf),
            vmem((5, 8, 128), f32),
            vmem((3, T, BLOCK, ROWS), bf),
            vmem((3, T, ROWS, BLOCK), bf),
            vmem((3, T, ROWS, 128), f32),
            vmem((2 * K, 1, CHUNK), f32),
            vmem((8, 128), f32),
            dma(K, 2), dma(K, 3),
            dma(5), dma(5), dma(K, 2, 5), dma(K, 2, 5), dma(K, 3), dma(K, 3),
            dma(T, K, 3), dma(T, K, 3), dma(T, K, 2), dma(T, K, 2),
            dma(T, 3, NX), dma(T, 3, NX), dma(T, NX), dma(T, NX),
            dma(T, K, 2), dma(T, K, 2), dma(T, K, 3), dma(T, K, 3),
            dma(K, 2, 3), dma(K, 2, 3), dma(K, 2, 2, 3), dma(K, 2, 2, 3),
        ],
        compiler_params=pltpu.CompilerParams(
            collective_id=0, has_side_effects=True, vmem_limit_bytes=50 * 2**20),
    )(forward_in[0], reverse_in[0], norm_gain, gate_up_weight[0], down_weight[0],
      expert_ids.reshape(2 * TICKS, 1, TOK), gate_weights.reshape(2 * TICKS, 1, TOK))
    return tuple(v[None] for v in outs)


def solution(mesh):
    in_specs = (
        P("section", "expert", None),
        P("section", "expert", None),
        P("section", None),
        P("section", None, None, "expert"),
        P("section", "expert", None),
        P("section", None, None, "expert", None),
        P("section", None, None, "expert", None),
    )
    out_specs = (P("section", "expert", None), P("section", "expert", None))
    return jax.shard_map(local, mesh=mesh, in_specs=in_specs, out_specs=out_specs, check_vma=False)
```
